256 devices in a mesh: dp: 8 (over x, core), seq: 32 (over y, z).
Axes of the slice: x: 4, y: 4, z: 8, core: 2. Of those that a mesh axis runs over, the one named last changes fastest.
Arguments:
- q_lin: bfloat16 [32768, 256], P(('dp', 'seq')), parts along dimension 0, may hold values from -9 to 9
- k_lin: bfloat16 [32768, 256], P(('dp', 'seq')), parts along dimension 0, may hold values from -9 to 9
- q_win: bfloat16 [32768, 1024], P(('dp', 'seq')), parts along dimension 0, may hold values from -6 to 6
- k_win: bfloat16 [32768, 1024], P(('dp', 'seq')), parts along dimension 0, may hold values from -6 to 6
- values: bfloat16 [32768, 1024], P(('dp', 'seq')), parts along dimension 0, may hold values from -8 to 8
- grad_out: bfloat16 [32768, 1024], P(('dp', 'seq')), parts along dimension 0, may hold values from -8 to 8
Outputs:
- mixed: bfloat16 [32768, 1024], P(('dp', 'seq')), parts along dimension 0
- grad_q_lin: bfloat16 [32768, 256], P(('dp', 'seq')), parts along dimension 0
- grad_k_lin: bfloat16 [32768, 256], P(('dp', 'seq')), parts along dimension 0
- grad_q_win: bfloat16 [32768, 1024], P(('dp', 'seq')), parts along dimension 0
- grad_k_win: bfloat16 [32768, 1024], P(('dp', 'seq')), parts along dimension 0
- grad_values: bfloat16 [32768, 1024], P(('dp', 'seq')), parts along dimension 0
The draws below stay inside these ranges and needn't reach their ends.
There are 8 independent parts, one for each index of `dp`. The reference program is written for one: setup_inputs(seed, part) draws one part's arguments, and reference() takes and returns one part's arrays. A program takes and returns all parts, laid end to end along the dimension named above; each array names one. Nothing has to cross between parts.
All inputs are finite; a program needn't handle non-finite values.
Results may differ from the reference program's by a relative error of at most 0.0091.
Values may be sent and summed in bfloat16 or wider, within the bound.
No kernel may reach another device: no remote copies, remote signals or barrier semaphores. Data moves between devices by JAX's collectives and lax.ppermute only.
A program may use at most 192 MiB of HBM per device.

```python
import math
import jax
import jax.numpy as jnp
from jax import lax

H = 16
DH = 64
FD = 16
WINDOW = 128
TOK_DEV = 128
SEQ_LEN = 4096


def window_jitter(key):
    row_width = H * DH
    jitter = jnp.clip(jax.random.normal(key, (SEQ_LEN, row_width)), -6.0, 6.0)
    return jitter


def draw_q_win(key, part):
    jitter = window_jitter(jax.random.fold_in(key, 11))
    result = jitter
    return result.astype(jnp.bfloat16)


def draw_k_win(key, part):
    jitter = window_jitter(jax.random.fold_in(key, 13))
    result = jitter
    return result.astype(jnp.bfloat16)


def shifted_field(key):
    row_width = H * DH
    segment = max(TOK_DEV // 4, 1)
    levels = jax.random.uniform(jax.random.fold_in(key, 3), (SEQ_LEN // segment + 1, row_width), minval=-2.0, maxval=2.0)
    level_rows = jnp.repeat(levels, segment, axis=0)[:SEQ_LEN]
    jitter = jnp.clip(jax.random.normal(jax.random.fold_in(key, 6), (SEQ_LEN, row_width)), -5.0, 5.0)
    return level_rows + jitter


def draw_values(key, part):
    return shifted_field(jax.random.fold_in(key, 21)).astype(jnp.bfloat16)


def draw_grad_out(key, part):
    return shifted_field(jax.random.fold_in(key, 22)).astype(jnp.bfloat16)


def shard_levels(stream_key, extent, pieces, low, top_value):
    def one(dim, shards_of):
        draws = jax.random.uniform(jax.random.fold_in(jax.random.fold_in(stream_key, 6), dim), (shards_of,), jnp.float32, low / len(pieces), top_value / len(pieces))
        return jnp.repeat(jnp.exp(draws), extent[dim] // shards_of).reshape((-1,) + (1,) * (len(extent) - dim - 1))

    factor_of = one(*pieces[0])
    for cut in pieces[1:]:
        factor_of = factor_of * one(*cut)
    return factor_of


def gaussian(own_key, shape, scale, limit, pieces=(), kind=jnp.bfloat16):
    values = scale * jax.random.normal(own_key, shape, jnp.float32)
    if pieces:
        values = values * shard_levels(own_key, shape, pieces, -0.22, 0.18)
    return jnp.clip(values, -limit, limit).astype(kind)


def setup_inputs(seed: int = 0, part: int = 0) -> dict:
    streams_of = jax.random.split(jax.random.key(seed), 7)
    own_keys = jax.random.split(jax.random.fold_in(streams_of[6], part), 7)
    return {
        "q_lin": gaussian(own_keys[0], (SEQ_LEN, H * FD), 1.5, 9.0, ((0, 32),)),
        "k_lin": gaussian(own_keys[1], (SEQ_LEN, H * FD), 1.5, 9.0, ((0, 32),)),
        "q_win": draw_q_win(jax.random.fold_in(jax.random.fold_in(streams_of[6], part), 71), part),
        "k_win": draw_k_win(jax.random.fold_in(jax.random.fold_in(streams_of[6], part), 71), part),
        "values": draw_values(jax.random.fold_in(jax.random.fold_in(streams_of[6], part), 71), part),
        "grad_out": draw_grad_out(jax.random.fold_in(jax.random.fold_in(streams_of[6], part), 71), part),
    }


HIGH = lax.Precision.HIGHEST

def feat_full(inputs):
    feat_depth = inputs.shape[-1]
    leading = inputs.shape[:-1]
    ones_col = jnp.ones(leading + (1,), inputs.dtype)
    square = (inputs[..., :, None] * inputs[..., None, :]).reshape(leading + (feat_depth * feat_depth,))
    linear_factor = 1.0 / math.sqrt(math.sqrt(feat_depth))
    return jnp.concatenate([ones_col, inputs * linear_factor, square / math.sqrt(2.0 * feat_depth)], -1)

def linear_pieces(lin_query, lin_key):
    inv_root = 1.0 / math.sqrt(lin_query.shape[-1])
    scores = jnp.einsum('thf,shf->hts', lin_query, lin_key, precision=HIGH) * inv_root
    tok_count = lin_query.shape[0]
    causal = jnp.arange(tok_count, dtype=jnp.int32)[:, None] >= jnp.arange(tok_count, dtype=jnp.int32)[None, :]
    kernel = jnp.where(causal[None], 1.0 + scores + 0.5 * scores * scores, 0.0)
    return (scores, kernel, causal)

def linear_grads(lin_query, lin_key, value_f32, d_numer, d_denom, prev_state, prev_norm, next_state, next_norm, scores, kernel, causal, key_feat, query_pull, key_pull):
    inv_root = 1.0 / math.sqrt(lin_query.shape[-1])
    d_kernel = jnp.einsum('thd,shd->hts', d_numer, value_f32, precision=HIGH) + d_denom.T[:, :, None]
    d_scores = jnp.where(causal[None], d_kernel, 0.0) * (1.0 + scores)
    d_values = jnp.einsum('hts,thd->shd', kernel, d_numer, precision=HIGH) + jnp.einsum('shf,hfd->shd', key_feat, next_state, precision=HIGH)
    d_qfeat = jnp.einsum('hfd,thd->thf', prev_state, d_numer, precision=HIGH) + prev_norm[None] * d_denom[:, :, None]
    d_kfeat = jnp.einsum('hfd,shd->shf', next_state, value_f32, precision=HIGH) + next_norm[None]
    d_query = jnp.einsum('hts,shf->thf', d_scores, lin_key, precision=HIGH) * inv_root + query_pull(d_qfeat)[0]
    d_key = jnp.einsum('hts,thf->shf', d_scores, lin_query, precision=HIGH) * inv_root + key_pull(d_kfeat)[0]
    return (d_query, d_key, d_values)

def window_block(query, key_rows, value_rows, grads, start):
    query = query.astype(jnp.float32)
    key_rows = key_rows.astype(jnp.float32)
    value_rows = value_rows.astype(jnp.float32)
    grads = grads.astype(jnp.float32)
    q_count = query.shape[0]
    k_count = key_rows.shape[0]
    inv_root = 1.0 / math.sqrt(query.shape[2])
    query_pos = start + jnp.arange(q_count, dtype=jnp.int32)[:, None]
    key_pos = start - (k_count - q_count) + jnp.arange(k_count, dtype=jnp.int32)[None, :]
    allowed = (key_pos <= query_pos) & (key_pos > query_pos - WINDOW) & (key_pos >= 0)
    logits = jnp.einsum('thd,shd->hts', query, key_rows, precision=HIGH) * inv_root
    logits = jnp.where(allowed[None], logits, -1e+30)
    shifted = jnp.exp(logits - lax.optimization_barrier(jnp.max(logits, -1, keepdims=True)))
    attn_weights = shifted / lax.optimization_barrier(jnp.sum(shifted, -1, keepdims=True))
    attn_low = lax.optimization_barrier(attn_weights.astype(jnp.bfloat16)).astype(jnp.float32)
    result = jnp.einsum('hts,shd->thd', attn_low, value_rows, precision=HIGH)
    d_attn = jnp.einsum('thd,shd->hts', grads, value_rows, precision=HIGH)
    d_values = jnp.einsum('hts,thd->shd', attn_low, grads, precision=HIGH)
    row_inner = lax.optimization_barrier(jnp.sum(grads * result, -1)).T
    d_logits = attn_weights * (d_attn - row_inner[:, :, None])
    d_logits = lax.optimization_barrier(d_logits.astype(jnp.bfloat16)).astype(jnp.float32)
    d_query = jnp.einsum('hts,shd->thd', d_logits, key_rows, precision=HIGH) * inv_root
    d_keys = jnp.einsum('hts,thd->shd', d_logits, query, precision=HIGH) * inv_root
    return (result, d_query, d_keys, d_values)

def reference(q_lin, k_lin, q_win, k_win, values, grad_out):
    total = q_lin.shape[0]
    blocks = total // TOK_DEV
    row_width = H * DH
    pad_keys = jnp.concatenate([jnp.zeros((WINDOW, row_width), k_win.dtype), k_win], 0)
    pad_values = jnp.concatenate([jnp.zeros((WINDOW, row_width), values.dtype), values], 0)

    def window_one(block_index):
        low_row = (block_index * TOK_DEV).astype(jnp.int32)
        return window_block(lax.dynamic_slice_in_dim(q_win, low_row, TOK_DEV, 0).reshape(TOK_DEV, H, DH), lax.dynamic_slice_in_dim(pad_keys, low_row, TOK_DEV + WINDOW, 0).reshape(TOK_DEV + WINDOW, H, DH), lax.dynamic_slice_in_dim(pad_values, low_row, TOK_DEV + WINDOW, 0).reshape(TOK_DEV + WINDOW, H, DH), lax.dynamic_slice_in_dim(grad_out, low_row, TOK_DEV, 0).reshape(TOK_DEV, H, DH), low_row)
    win_out, win_dq, win_dk, win_dv = lax.map(window_one, jnp.arange(blocks, dtype=jnp.int32))

    def settle(grads_all):
        own_part = grads_all[:, WINDOW:]
        moved = jnp.concatenate([grads_all[1:, :WINDOW], jnp.zeros_like(grads_all[:1, :WINDOW])], 0)
        return own_part.at[:, TOK_DEV - WINDOW:].add(moved)

    def split(array, feat_depth):
        return array.reshape(blocks, TOK_DEV, H, feat_depth).astype(jnp.float32)
    block_q = split(q_lin, FD)
    block_k = split(k_lin, FD)
    block_v = split(values, DH)
    block_g = split(grad_out, DH)
    feats = 1 + FD + FD * FD
    empty = (jnp.zeros((H, feats, DH), jnp.float32), jnp.zeros((H, feats), jnp.float32))

    def forward_step(carry, inputs):
        run_state, run_norm = carry
        lin_query, lin_key, value_f32 = inputs
        scores, kernel, causal = linear_pieces(lin_query, lin_key)
        query_feat = feat_full(lin_query)
        key_feat = feat_full(lin_key)
        numer = jnp.einsum('thf,hfd->thd', query_feat, run_state, precision=HIGH) + jnp.einsum('hts,shd->thd', kernel, value_f32, precision=HIGH)
        denom = jnp.einsum('thf,hf->th', query_feat, run_norm, precision=HIGH) + lax.optimization_barrier(jnp.sum(kernel, -1)).T
        own_state = jnp.einsum('thf,thd->hfd', key_feat, value_f32, precision=HIGH)
        own_norm = lax.optimization_barrier(jnp.sum(key_feat, 0))
        return ((run_state + own_state, run_norm + own_norm), (numer / denom[:, :, None], denom, run_state, run_norm))
    _, (lin_out, denom, prev_state, prev_norm) = lax.scan(forward_step, empty, (block_q, block_k, block_v))
    d_numer = block_g / denom[..., None]
    d_denom = -lax.optimization_barrier(jnp.sum(block_g * lin_out, -1)) / denom

    def backward_step(carry, inputs):
        run_state, run_norm = carry
        lin_query, numer_grad, denom_grad = inputs
        query_feat = feat_full(lin_query)
        own_state = jnp.einsum('thf,thd->hfd', query_feat, numer_grad, precision=HIGH)
        own_norm = jnp.einsum('thf,th->hf', query_feat, denom_grad, precision=HIGH)
        return ((run_state + own_state, run_norm + own_norm), (run_state, run_norm))
    _, (next_state, next_norm) = lax.scan(backward_step, empty, (block_q, d_numer, d_denom), reverse=True)

    def grad_one(inputs):
        lin_query, lin_key, value_f32, numer_grad, denom_grad, state_before, norm_before, state_after, norm_after = inputs
        scores, kernel, causal = linear_pieces(lin_query, lin_key)
        key_feat, key_pull = jax.vjp(feat_full, lin_key)
        query_feat, query_pull = jax.vjp(feat_full, lin_query)
        return linear_grads(lin_query, lin_key, value_f32, numer_grad, denom_grad, state_before, norm_before, state_after, norm_after, scores, kernel, causal, key_feat, query_pull, key_pull)
    lin_dq, lin_dk, lin_dv = lax.map(grad_one, (block_q, block_k, block_v, d_numer, d_denom, prev_state, prev_norm, next_state, next_norm))
    mixed = (lin_out.reshape(total, row_width) + win_out.reshape(total, row_width)).astype(jnp.bfloat16)
    grad_q_lin = lin_dq.reshape(total, H * FD).astype(jnp.bfloat16)
    grad_k_lin = lin_dk.reshape(total, H * FD).astype(jnp.bfloat16)
    grad_q_win = win_dq.reshape(total, row_width).astype(jnp.bfloat16)
    grad_k_win = settle(win_dk).reshape(total, row_width).astype(jnp.bfloat16)
    grad_values = (lin_dv.reshape(total, row_width) + settle(win_dv).reshape(total, row_width)).astype(jnp.bfloat16)
    return (mixed, grad_q_lin, grad_k_lin, grad_q_win, grad_k_win, grad_values)
```

```python
import functools

import jax
import jax.numpy as jnp
from jax import lax
from jax.experimental import pallas as pl
from jax.experimental.pallas import tpu as pltpu
from jax.sharding import Mesh, PartitionSpec as P

H = 16
DH = 64
FD = 16
TOK = 128
FEAT = 224
ROWS = 80
WIDE = 256
STEPS = 8
BF = jnp.bfloat16
F32 = jnp.float32
PARAMS = pltpu.CompilerParams(vmem_limit_bytes=16 * 1024 * 1024)


def nn(a, b):
    return lax.dot_general(a, b, (((1,), (0,)), ((), ())), preferred_element_type=F32)


def nt(a, b):
    return lax.dot_general(a, b, (((1,), (1,)), ((), ())), preferred_element_type=F32)


def split(x):
    high = x.astype(BF)
    return high, (x - high.astype(F32)).astype(BF)


def flip(x):
    return jnp.transpose(x.astype(F32)).astype(BF)


def pack_kernel(
    ql_hbm, kl_hbm, kw_hbm, v_hbm, g_hbm, out_ref, halo_hbm,
    ql_ref, kl_ref, kw_ref, v_ref, g_ref, sems,
):
    def copy(source, target, i):
        job = pltpu.make_async_copy(source, target, sems.at[i])
        job.start()
        return job

    value_in = copy(v_hbm, v_ref, 0)
    window_in = copy(kw_hbm, kw_ref, 1)
    grad_in = copy(g_hbm, g_ref, 2)
    key_in = copy(kl_hbm, kl_ref, 3)
    query_in = copy(ql_hbm, ql_ref, 4)
    value_in.wait()
    value_out = copy(v_ref, halo_hbm.at[1], 5)
    window_in.wait()
    window_out = copy(kw_ref, halo_hbm.at[0], 6)

    def wide(ref, base):
        for p in range(8):
            part = flip(ref[:, p * 128 : (p + 1) * 128])
            out_ref[2 * p, base : base + 64, :] = part[0:64]
            out_ref[2 * p + 1, base : base + 64, :] = part[64:128]

    def thin(ref, base):
        for j in range(2):
            part = flip(ref[:, j * 128 : (j + 1) * 128])
            for i in range(8):
                out_ref[8 * j + i, base : base + 16, :] = part[16 * i : 16 * i + 16]

    wide(v_ref, 16)
    grad_in.wait()
    wide(g_ref, 96)
    key_in.wait()
    thin(kl_ref, 0)
    query_in.wait()
    thin(ql_ref, 80)
    value_out.wait()
    window_out.wait()


def pack(q_lin, k_lin, k_win, values, grad_out):
    hbm = pl.BlockSpec(memory_space=pltpu.HBM)
    return pl.pallas_call(
        pack_kernel,
        in_specs=[hbm] * 5,
        out_specs=(pl.BlockSpec(memory_space=pltpu.VMEM), hbm),
        out_shape=(
            jax.ShapeDtypeStruct((H, 2 * ROWS, TOK), BF),
            jax.ShapeDtypeStruct((2, TOK, H * DH), BF),
        ),
        scratch_shapes=[
            pltpu.VMEM((TOK, H * FD), BF),
            pltpu.VMEM((TOK, H * FD), BF),
            pltpu.VMEM((TOK, H * DH), BF),
            pltpu.VMEM((TOK, H * DH), BF),
            pltpu.VMEM((TOK, H * DH), BF),
            pltpu.SemaphoreType.DMA((7,)),
        ],
        compiler_params=pltpu.CompilerParams(vmem_limit_bytes=60 * 1024 * 1024),
        name="pack",
    )(q_lin, k_lin, k_win, values, grad_out)


def features(x, square=1.0, cross=1.0, linear=1.0):
    low, up = x[0:8], x[8:16]
    left, mix, right = low * square, up * cross, up * square
    pieces = []
    for i in range(8):
        row = x[i : i + 1]
        pieces += [row * left, row * mix]
    for i in range(8, 16):
        pieces.append(x[i : i + 1] * right)
    pieces += [low * linear, up * linear]
    one = (lax.broadcasted_iota(jnp.int32, (8, x.shape[1]), 0) == 0).astype(F32)
    pieces += [one, jnp.zeros_like(one)]
    return jnp.concatenate(pieces, 0).astype(BF)


def pull(x, grad, weight):
    low, up = x[0:8], x[8:16]
    row_id = lax.broadcasted_iota(jnp.int32, low.shape, 0)
    acc_low = jnp.zeros_like(low)
    acc_mix = jnp.zeros_like(low)
    acc_up = jnp.zeros_like(low)
    red = jnp.zeros_like(low)
    for i in range(8):
        row = x[i : i + 1]
        own = grad[16 * i : 16 * i + 8]
        mix = grad[16 * i + 8 : 16 * i + 16]
        acc_low = acc_low + row * own
        acc_mix = acc_mix + row * mix
        red = jnp.where(row_id == i, jnp.sum(up * mix, 0, keepdims=True), red)
    for i in range(8, 16):
        acc_up = acc_up + x[i : i + 1] * grad[128 + 8 * (i - 8) : 136 + 8 * (i - 8)]
    if weight:
        out_low = (acc_low + red) * (1.0 / 16.0) + grad[192:200] * 0.25
        out_up = (acc_mix + acc_up) * (1.0 / 16.0) + grad[200:208] * 0.25
    else:
        out_low = 2.0 * acc_low + red + grad[192:200]
        out_up = acc_mix + 2.0 * acc_up + grad[200:208]
    return jnp.concatenate([out_low, out_up], 0)


def rows_of(ref, c, start, stop):
    return jnp.concatenate([ref[2 * c, start:stop], ref[2 * c + 1, start:stop]], 1)


def with_ones(v):
    tail = (lax.broadcasted_iota(jnp.int32, (16, v.shape[1]), 0) == 0).astype(BF)
    return jnp.concatenate([v, tail], 0)


def state_kernel(x_ref, pref_ref, total_ref, feat_ref):
    run = jnp.zeros((ROWS, FEAT), F32)
    for c in range(STEPS):
        pref_ref[c] = run
        key = rows_of(x_ref, c, 0, 16).astype(F32)
        feat = features(key, 1.0 / 32.0, 1.0 / 16.0, 0.25)
        feat_ref[c] = feat
        ones = with_ones(rows_of(x_ref, c, 16, 80))
        run = run + nt(ones, feat)
    total_ref[...] = run


def key_state(x):
    feat = jax.ShapeDtypeStruct((STEPS, FEAT, WIDE), BF)
    return pl.pallas_call(
        state_kernel,
        out_shape=(
            jax.ShapeDtypeStruct((STEPS, ROWS, FEAT), F32),
            jax.ShapeDtypeStruct((ROWS, FEAT), F32),
            feat,
        ),
        compiler_params=PARAMS,
        name="key_state",
    )(x)


def causal_mask():
    source = lax.broadcasted_iota(jnp.int32, (WIDE, WIDE), 0)
    target = lax.broadcasted_iota(jnp.int32, (WIDE, WIDE), 1)
    return source <= target


def inside_kernel(x_ref, scores_ref, numer_ref, feat_ref):
    causal = causal_mask()
    for c in range(STEPS):
        key = rows_of(x_ref, c, 0, 16)
        query = rows_of(x_ref, c, 80, 96)
        ones = with_ones(rows_of(x_ref, c, 16, 80))
        scores = nn(flip(key), query) * 0.25
        scores_ref[c] = scores
        kernel_hi, kernel_lo = split(
            jnp.where(causal, 1.0 + scores + 0.5 * scores * scores, 0.0)
        )
        numer_ref[c] = nn(ones, kernel_hi) + nn(ones, kernel_lo)
        feat_ref[c] = features(query.astype(F32))


def inside(x):
    feat = jax.ShapeDtypeStruct((STEPS, FEAT, WIDE), BF)
    return pl.pallas_call(
        inside_kernel,
        out_shape=(
            jax.ShapeDtypeStruct((STEPS, WIDE, WIDE), F32),
            jax.ShapeDtypeStruct((STEPS, ROWS, WIDE), F32),
            feat,
        ),
        compiler_params=PARAMS,
        name="inside_chunks",
    )(x)


def output_kernel(
    x_ref, pref_ref, half_ref, numer_ref, feat_ref,
    lin_ref, dhi_ref, dlo_ref, own_ref, total_ref,
):
    total = jnp.zeros((ROWS, FEAT), F32)
    first = lax.broadcasted_iota(jnp.int32, (16, WIDE), 0) == 0
    for c in range(STEPS):
        grads = rows_of(x_ref, c, 96, 160).astype(F32)
        feat = feat_ref[c]
        state_hi, state_lo = split(pref_ref[c] + half_ref[...])
        stack = nn(jnp.concatenate([state_hi, state_lo], 0), feat)
        numer = numer_ref[c] + stack[0:ROWS] + stack[ROWS:]
        inv = 1.0 / numer[64:65]
        lin_out = numer[0:64] * inv
        d_denom = -jnp.sum(grads * lin_out, 0, keepdims=True) * inv
        d_hi, d_lo = split(
            jnp.concatenate([grads * inv, jnp.where(first, d_denom, 0.0)], 0)
        )
        stack = nt(jnp.concatenate([d_hi, d_lo], 0), feat)
        own = stack[0:ROWS] + stack[ROWS:]
        own_ref[c] = own
        total = total + own
        lin_ref[c] = lin_out.astype(BF)
        dhi_ref[c] = d_hi
        dlo_ref[c] = d_lo
    total_ref[...] = total


def output(x, pref, half, numer, feat):
    side = jax.ShapeDtypeStruct((STEPS, ROWS, WIDE), BF)
    return pl.pallas_call(
        output_kernel,
        out_shape=(
            jax.ShapeDtypeStruct((STEPS, DH, WIDE), BF),
            side,
            side,
            jax.ShapeDtypeStruct((STEPS, ROWS, FEAT), F32),
            jax.ShapeDtypeStruct((ROWS, FEAT), F32),
        ),
        compiler_params=PARAMS,
        name="linear_output",
    )(x, pref, half, numer, feat)


def query_kernel(x_ref, scores_ref, pref_ref, half_ref, dhi_ref, dlo_ref, dq_ref, part_ref):
    causal = causal_mask()
    for c in range(STEPS):
        key = rows_of(x_ref, c, 0, 16)
        query = rows_of(x_ref, c, 80, 96)
        ones_t = flip(with_ones(rows_of(x_ref, c, 16, 80)))
        d_hi, d_lo = dhi_ref[c], dlo_ref[c]
        scores = scores_ref[c]
        kernel = jnp.where(causal, 1.0 + scores + 0.5 * scores * scores, 0.0).astype(BF)
        turned_hi, turned_lo = split(jnp.transpose(pref_ref[c] + half_ref[...]))
        d_feat = nn(turned_hi, d_hi) + nn(turned_lo, d_hi) + nn(turned_hi, d_lo)
        d_kernel = nn(ones_t, d_hi) + nn(ones_t, d_lo)
        d_scores = jnp.where(causal, d_kernel * (1.0 + scores), 0.0).astype(BF)
        d_query = pull(query.astype(F32), d_feat, False) + nn(key, d_scores) * 0.25
        dq_ref[c] = d_query.astype(BF)
        part_ref[c, 0:64] = nt(d_hi[0:64], kernel)
        part_ref[c, 64:80] = nt(query, d_scores) * 0.25


def query_grads(x, scores, pref, half, d_hi, d_lo):
    return pl.pallas_call(
        query_kernel,
        out_shape=(
            jax.ShapeDtypeStruct((STEPS, FD, WIDE), BF),
            jax.ShapeDtypeStruct((STEPS, ROWS, WIDE), F32),
        ),
        compiler_params=PARAMS,
        name="query_grads",
    )(x, scores, pref, half, d_hi, d_lo)


def key_kernel(x_ref, lin_ref, dq_ref, part_ref, own_ref, half_ref, feat_ref, out_ref):
    run = half_ref[...]
    for c in range(STEPS - 1, -1, -1):
        key = rows_of(x_ref, c, 0, 16).astype(F32)
        ones = with_ones(rows_of(x_ref, c, 16, 80))
        feat = feat_ref[c]
        run_hi, run_lo = split(run)
        stack = nn(jnp.concatenate([run_hi[0:64], run_lo[0:64]], 0), feat)
        d_value = stack[0:64] + stack[64:128] + part_ref[c, 0:64]
        turned_hi, turned_lo = split(jnp.transpose(run))
        d_feat = nn(turned_hi, ones) + nn(turned_lo, ones)
        d_key = (pull(key, d_feat, True) + part_ref[c, 64:80]).astype(BF)
        d_value = d_value.astype(BF)
        for i in range(2):
            cols = slice(i * TOK, (i + 1) * TOK)
            out_ref[2 * c + i, 0:64] = lin_ref[c, :, cols]
            out_ref[2 * c + i, 64:80] = dq_ref[c, :, cols]
            out_ref[2 * c + i, 80:144] = d_value[:, cols]
            out_ref[2 * c + i, 144:160] = d_key[:, cols]
        if c:
            run = run + own_ref[c]


def key_grads(x, lin, dq, part, own, half, feat):
    return pl.pallas_call(
        key_kernel,
        out_shape=jax.ShapeDtypeStruct((H, 2 * ROWS, TOK), BF),
        compiler_params=PARAMS,
        name="key_grads",
    )(x, lin, dq, part, own, half, feat)


def window_kernel(
    first_ref, q_ref, k_ref, v_ref, g_ref, halo_ref,
    out_ref, dq_ref, dk_ref, dv_ref, back_hbm, back_ref, sems,
):
    source = lax.broadcasted_iota(jnp.int32, (TOK, 2 * TOK), 0)
    target = lax.broadcasted_iota(jnp.int32, (TOK, 2 * TOK), 1) % TOK
    own = source <= target
    own_low = own.astype(F32).astype(BF)
    prev_low = (1.0 - own.astype(F32)).astype(BF)
    row = lax.broadcasted_iota(jnp.int32, (TOK, TOK), 0)
    col = lax.broadcasted_iota(jnp.int32, (TOK, TOK), 1)
    own_t = (col <= row).astype(F32).astype(BF)
    prev_t = (col > row).astype(F32).astype(BF)
    lane_a = (col < DH).astype(F32).astype(BF)
    lane_b = (col >= DH).astype(F32).astype(BF)
    blocked = jnp.where(first_ref[0] == 1, -1e30, 0.0)

    def both(x):
        return jnp.concatenate([x * lane_a, x * lane_b], 0)

    copies = []
    for p in range(H // 2):
        cols = slice(p * 128, (p + 1) * 128)
        key, key_p = k_ref[:, cols], halo_ref[0, :, cols]
        value, value_p = v_ref[:, cols], halo_ref[1, :, cols]
        query2 = both(q_ref[:, cols])
        grad2 = both(g_ref[:, cols])
        logits = jnp.where(own, nt(key, query2) * 0.125, nt(key_p, query2) * 0.125 + blocked)
        shifted = jnp.exp(logits - jnp.max(logits, 0, keepdims=True))
        attn = shifted * (1.0 / jnp.sum(shifted, 0, keepdims=True))
        attn_low = attn.astype(BF)
        pieces = []
        for i in range(2):
            turned = flip(attn_low[:, i * TOK : (i + 1) * TOK])
            pieces += [turned * own_t, turned * prev_t]
        values4 = jnp.concatenate(
            [value * lane_a, value_p * lane_a, value * lane_b, value_p * lane_b], 0
        )
        result = nn(jnp.concatenate(pieces, 1), values4)
        out_ref[:, cols] = result
        inner_t = jnp.transpose(result * g_ref[:, cols].astype(F32))
        inner = jnp.concatenate(
            [jnp.sum(inner_t[0:64], 0, keepdims=True), jnp.sum(inner_t[64:128], 0, keepdims=True)],
            1,
        )
        d_attn = jnp.where(own, nt(value, grad2), nt(value_p, grad2))
        d_logits = (attn * (d_attn - inner)).astype(BF)
        pieces = []
        for i in range(2):
            turned = flip(d_logits[:, i * TOK : (i + 1) * TOK])
            pieces += [turned * own_t, turned * prev_t]
        keys4 = jnp.concatenate([key * lane_a, key_p * lane_a, key * lane_b, key_p * lane_b], 0)
        dq_ref[:, cols] = (nn(jnp.concatenate(pieces, 1), keys4) * 0.125).astype(BF)
        dk_ref[:, cols] = nn(d_logits * own_low, query2) * 0.125
        back_ref[0, :, cols] = (nn(d_logits * prev_low, query2) * 0.125).astype(BF)
        dv_ref[:, cols] = nn(attn_low * own_low, grad2)
        back_ref[1, :, cols] = nn(attn_low * prev_low, grad2).astype(BF)
        copies.append(
            pltpu.make_async_copy(back_ref.at[:, :, cols], back_hbm.at[:, :, cols], sems.at[p])
        )
        copies[-1].start()
    for copy in copies:
        copy.wait()


def window(first, q, k, v, g, halo):
    wide = (TOK, H * DH)
    vmem = pl.BlockSpec(memory_space=pltpu.VMEM)
    return pl.pallas_call(
        window_kernel,
        in_specs=[pl.BlockSpec(memory_space=pltpu.SMEM)] + [vmem] * 5,
        out_specs=(vmem,) * 4 + (pl.BlockSpec(memory_space=pltpu.HBM),),
        out_shape=(
            jax.ShapeDtypeStruct(wide, F32),
            jax.ShapeDtypeStruct(wide, BF),
            jax.ShapeDtypeStruct(wide, F32),
            jax.ShapeDtypeStruct(wide, F32),
            jax.ShapeDtypeStruct((2,) + wide, BF),
        ),
        scratch_shapes=[pltpu.VMEM((2,) + wide, BF), pltpu.SemaphoreType.DMA((8,))],
        compiler_params=PARAMS,
        cost_estimate=pl.CostEstimate(
            flops=50_000_000_000, transcendentals=0, bytes_accessed=6_000_000
        ),
        name="window",
    )(first, q, k, v, g, halo)


def finish_kernel(
    y_ref, out_ref, dk_ref, dv_ref, halo_ref, mixed_ref, gq_ref, gk_ref, gkw_ref, gv_ref
):
    for p in range(8):
        cols = slice(p * 128, (p + 1) * 128)
        pair = jnp.concatenate([y_ref[2 * p, 0:64], y_ref[2 * p + 1, 0:64]], 0)
        mixed_ref[:, cols] = (jnp.transpose(pair.astype(F32)) + out_ref[:, cols]).astype(BF)
        pair = jnp.concatenate([y_ref[2 * p, 80:144], y_ref[2 * p + 1, 80:144]], 0)
        own = dv_ref[:, cols] + halo_ref[1, :, cols].astype(F32)
        gv_ref[:, cols] = (jnp.transpose(pair.astype(F32)) + own).astype(BF)
        gkw_ref[:, cols] = (dk_ref[:, cols] + halo_ref[0, :, cols].astype(F32)).astype(BF)
    for j in range(2):
        cols = slice(j * 128, (j + 1) * 128)
        for ref, row in ((gq_ref, 64), (gk_ref, 144)):
            ref[:, cols] = flip(
                jnp.concatenate([y_ref[8 * j + i, row : row + 16] for i in range(8)], 0)
            )


def finish(y, out, dk, dv, halo):
    wide = jax.ShapeDtypeStruct((TOK, H * DH), BF)
    thin = jax.ShapeDtypeStruct((TOK, H * FD), BF)
    return pl.pallas_call(
        finish_kernel,
        out_shape=(wide, thin, thin, wide, wide),
        compiler_params=PARAMS,
        name="finish",
    )(y, out, dk, dv, halo)


def local(q_lin, k_lin, q_win, k_win, values, grad_out):
    seq = ("half", "head")
    spread = functools.partial(
        lax.all_to_all, axis_name="head", split_axis=0, concat_axis=0, tiled=True
    )
    later = [(i, i + 1) for i in range(31)]
    earlier = [(i + 1, i) for i in range(31)]
    own, halo = pack(q_lin, k_lin, k_win, values, grad_out)
    halo = lax.ppermute(halo, seq, later)
    x = spread(own)
    first = (lax.axis_index(seq) == 0).astype(jnp.int32).reshape(1)
    out, dq_win, dk, dv, back_halo = window(first, q_win, k_win, values, grad_out, halo)
    back_halo = lax.ppermute(back_halo, seq, earlier)
    x, dk, dv = lax.optimization_barrier((x, dk, dv))
    pref, total, key_feat = key_state(x)
    half = lax.ppermute(total, "half", [(0, 1)])
    scores, numer, query_feat = inside(x)
    numer, half = lax.optimization_barrier((numer, half))
    lin, d_hi, d_lo, state, total = output(x, pref, half, numer, query_feat)
    next_half = lax.ppermute(total, "half", [(1, 0)])
    dq, part = query_grads(x, scores, pref, half, d_hi, d_lo)
    dq, back_halo = lax.optimization_barrier((dq, back_halo))
    y = spread(key_grads(x, lin, dq, part, state, next_half, key_feat))
    mixed, gq, gk, gkw, gv = finish(y, out, dk, dv, back_halo)
    return (mixed, gq, gk, dq_win, gkw, gv)


def solution(mesh):
    inner = Mesh(mesh.devices.reshape(8, 2, 16), ("dp", "half", "head"))
    placed = P(("dp", "half", "head"), None)
    return jax.shard_map(
        local, mesh=inner, in_specs=(placed,) * 6, out_specs=(placed,) * 6, check_vma=False
    )
```

```python
import functools

import jax
import jax.numpy as jnp
from jax import lax
from jax.experimental import pallas as pl
from jax.experimental.pallas import tpu as pltpu
from jax.sharding import Mesh, PartitionSpec as P

H = 16
DH = 64
FD = 16
TOK = 128
FEAT = 224
ROWS = 80
WIDE = 256
STEPS = 8
BF = jnp.bfloat16
F32 = jnp.float32
PARAMS = pltpu.CompilerParams(vmem_limit_bytes=16 * 1024 * 1024)


def nn(a, b):
    return lax.dot_general(a, b, (((1,), (0,)), ((), ())), preferred_element_type=F32)


def nt(a, b):
    return lax.dot_general(a, b, (((1,), (1,)), ((), ())), preferred_element_type=F32)


def split(x):
    high = x.astype(BF)
    return high, (x - high.astype(F32)).astype(BF)


def flip(x):
    return jnp.transpose(x)


def pack_kernel(
    ql_hbm, kl_hbm, kw_hbm, v_hbm, g_hbm, out_ref, halo_hbm,
    ql_ref, kl_ref, kw_ref, v_ref, g_ref, sems,
):
    def copy(source, target, i):
        job = pltpu.make_async_copy(source, target, sems.at[i])
        job.start()
        return job

    value_in = copy(v_hbm, v_ref, 0)
    window_in = copy(kw_hbm, kw_ref, 1)
    grad_in = copy(g_hbm, g_ref, 2)
    key_in = copy(kl_hbm, kl_ref, 3)
    query_in = copy(ql_hbm, ql_ref, 4)
    value_in.wait()
    value_out = copy(v_ref, halo_hbm.at[1], 5)
    window_in.wait()
    window_out = copy(kw_ref, halo_hbm.at[0], 6)

    def wide(ref, base):
        for p in range(8):
            part = flip(ref[:, p * 128 : (p + 1) * 128])
            out_ref[2 * p, base : base + 64, :] = part[0:64]
            out_ref[2 * p + 1, base : base + 64, :] = part[64:128]

    def thin(ref, base):
        for j in range(2):
            part = flip(ref[:, j * 128 : (j + 1) * 128])
            for i in range(8):
                out_ref[8 * j + i, base : base + 16, :] = part[16 * i : 16 * i + 16]

    wide(v_ref, 16)
    grad_in.wait()
    wide(g_ref, 96)
    key_in.wait()
    thin(kl_ref, 0)
    query_in.wait()
    thin(ql_ref, 80)
    value_out.wait()
    window_out.wait()


def pack(q_lin, k_lin, k_win, values, grad_out):
    hbm = pl.BlockSpec(memory_space=pltpu.HBM)
    return pl.pallas_call(
        pack_kernel,
        in_specs=[hbm] * 5,
        out_specs=(pl.BlockSpec(memory_space=pltpu.VMEM), hbm),
        out_shape=(
            jax.ShapeDtypeStruct((H, 2 * ROWS, TOK), BF),
            jax.ShapeDtypeStruct((2, TOK, H * DH), BF),
        ),
        scratch_shapes=[
            pltpu.VMEM((TOK, H * FD), BF),
            pltpu.VMEM((TOK, H * FD), BF),
            pltpu.VMEM((TOK, H * DH), BF),
            pltpu.VMEM((TOK, H * DH), BF),
            pltpu.VMEM((TOK, H * DH), BF),
            pltpu.SemaphoreType.DMA((7,)),
        ],
        compiler_params=pltpu.CompilerParams(vmem_limit_bytes=60 * 1024 * 1024),
        name="pack",
    )(q_lin, k_lin, k_win, values, grad_out)


def features(x, square=1.0, cross=1.0, linear=1.0):
    low, up = x[0:8], x[8:16]
    left, mix, right = low * square, up * cross, up * square
    pieces = []
    for i in range(8):
        row = x[i : i + 1]
        pieces += [row * left, row * mix]
    for i in range(8, 16):
        pieces.append(x[i : i + 1] * right)
    pieces += [low * linear, up * linear]
    one = (lax.broadcasted_iota(jnp.int32, (8, x.shape[1]), 0) == 0).astype(F32)
    pieces += [one, jnp.zeros_like(one)]
    return jnp.concatenate(pieces, 0).astype(BF)


def pull(x, grad, weight):
    low, up = x[0:8], x[8:16]
    row_id = lax.broadcasted_iota(jnp.int32, low.shape, 0)
    acc_low = jnp.zeros_like(low)
    acc_mix = jnp.zeros_like(low)
    acc_up = jnp.zeros_like(low)
    red = jnp.zeros_like(low)
    for i in range(8):
        row = x[i : i + 1]
        own = grad[16 * i : 16 * i + 8]
        mix = grad[16 * i + 8 : 16 * i + 16]
        acc_low = acc_low + row * own
        acc_mix = acc_mix + row * mix
        red = jnp.where(row_id == i, jnp.sum(up * mix, 0, keepdims=True), red)
    for i in range(8, 16):
        acc_up = acc_up + x[i : i + 1] * grad[128 + 8 * (i - 8) : 136 + 8 * (i - 8)]
    if weight:
        out_low = (acc_low + red) * (1.0 / 16.0) + grad[192:200] * 0.25
        out_up = (acc_mix + acc_up) * (1.0 / 16.0) + grad[200:208] * 0.25
    else:
        out_low = 2.0 * acc_low + red + grad[192:200]
        out_up = acc_mix + 2.0 * acc_up + grad[200:208]
    return jnp.concatenate([out_low, out_up], 0)


def rows_of(ref, c, start, stop):
    return jnp.concatenate([ref[2 * c, start:stop], ref[2 * c + 1, start:stop]], 1)


def with_ones(v):
    tail = (lax.broadcasted_iota(jnp.int32, (16, v.shape[1]), 0) == 0).astype(BF)
    return jnp.concatenate([v, tail], 0)


def state_kernel(x_ref, pref_ref, total_ref, feat_ref):
    run = jnp.zeros((ROWS, FEAT), F32)
    for c in range(STEPS):
        pref_ref[c] = run
        key = rows_of(x_ref, c, 0, 16).astype(F32)
        feat = features(key, 1.0 / 32.0, 1.0 / 16.0, 0.25)
        feat_ref[c] = feat
        ones = with_ones(rows_of(x_ref, c, 16, 80))
        run = run + nt(ones, feat)
    total_ref[...] = run


def key_state(x):
    feat = jax.ShapeDtypeStruct((STEPS, FEAT, WIDE), BF)
    return pl.pallas_call(
        state_kernel,
        out_shape=(
            jax.ShapeDtypeStruct((STEPS, ROWS, FEAT), F32),
            jax.ShapeDtypeStruct((ROWS, FEAT), F32),
            feat,
        ),
        compiler_params=PARAMS,
        name="key_state",
    )(x)


def causal_mask():
    source = lax.broadcasted_iota(jnp.int32, (WIDE, WIDE), 0)
    target = lax.broadcasted_iota(jnp.int32, (WIDE, WIDE), 1)
    return source <= target


def inside_kernel(x_ref, scores_ref, numer_ref, feat_ref):
    causal = causal_mask()
    for c in range(STEPS):
        key = rows_of(x_ref, c, 0, 16)
        query = rows_of(x_ref, c, 80, 96)
        ones = with_ones(rows_of(x_ref, c, 16, 80))
        scores = nn(flip(key), query) * 0.25
        scores_ref[c] = scores
        kernel_hi, kernel_lo = split(
            jnp.where(causal, 1.0 + scores + 0.5 * scores * scores, 0.0)
        )
        numer_ref[c] = nn(ones, kernel_hi) + nn(ones, kernel_lo)
        feat_ref[c] = features(query.astype(F32))


def inside(x):
    feat = jax.ShapeDtypeStruct((STEPS, FEAT, WIDE), BF)
    return pl.pallas_call(
        inside_kernel,
        out_shape=(
            jax.ShapeDtypeStruct((STEPS, WIDE, WIDE), F32),
            jax.ShapeDtypeStruct((STEPS, ROWS, WIDE), F32),
            feat,
        ),
        compiler_params=PARAMS,
        name="inside_chunks",
    )(x)


def output_kernel(
    x_ref, pref_ref, half_ref, numer_ref, feat_ref,
    lin_ref, dhi_ref, dlo_ref, own_ref, total_ref,
):
    total = jnp.zeros((ROWS, FEAT), F32)
    first = lax.broadcasted_iota(jnp.int32, (16, WIDE), 0) == 0
    for c in range(STEPS):
        grads = rows_of(x_ref, c, 96, 160).astype(F32)
        feat = feat_ref[c]
        state_hi, state_lo = split(pref_ref[c] + half_ref[...])
        stack = nn(jnp.concatenate([state_hi, state_lo], 0), feat)
        numer = numer_ref[c] + stack[0:ROWS] + stack[ROWS:]
        inv = 1.0 / numer[64:65]
        lin_out = numer[0:64] * inv
        d_denom = -jnp.sum(grads * lin_out, 0, keepdims=True) * inv
        d_hi, d_lo = split(
            jnp.concatenate([grads * inv, jnp.where(first, d_denom, 0.0)], 0)
        )
        stack = nt(jnp.concatenate([d_hi, d_lo], 0), feat)
        own = stack[0:ROWS] + stack[ROWS:]
        own_ref[c] = own
        total = total + own
        lin_ref[c] = lin_out.astype(BF)
        dhi_ref[c] = d_hi
        dlo_ref[c] = d_lo
    total_ref[...] = total


def output(x, pref, half, numer, feat):
    side = jax.ShapeDtypeStruct((STEPS, ROWS, WIDE), BF)
    return pl.pallas_call(
        output_kernel,
        out_shape=(
            jax.ShapeDtypeStruct((STEPS, DH, WIDE), BF),
            side,
            side,
            jax.ShapeDtypeStruct((STEPS, ROWS, FEAT), F32),
            jax.ShapeDtypeStruct((ROWS, FEAT), F32),
        ),
        compiler_params=PARAMS,
        name="linear_output",
    )(x, pref, half, numer, feat)


def query_kernel(
    x_ref, scores_ref, pref_ref, half_ref, dhi_ref, dlo_ref, dq_ref, part_ref,
    feat_ref, low_ref,
):
    causal = causal_mask()
    for c in range(STEPS):
        d_hi, d_lo = dhi_ref[c], dlo_ref[c]
        ones_t = flip(with_ones(rows_of(x_ref, c, 16, 80)))
        d_kernel = nn(ones_t, d_hi) + nn(ones_t, d_lo)
        low_ref[c] = jnp.where(causal, d_kernel * (1.0 + scores_ref[c]), 0.0).astype(BF)
    for c in range(STEPS):
        d_hi, d_lo = dhi_ref[c], dlo_ref[c]
        turned_hi, turned_lo = split(jnp.transpose(pref_ref[c] + half_ref[...]))
        feat_ref[c] = nn(turned_hi, d_hi) + nn(turned_lo, d_hi) + nn(turned_hi, d_lo)
    for c in range(STEPS):
        scores = scores_ref[c]
        kernel = jnp.where(causal, 1.0 + scores + 0.5 * scores * scores, 0.0).astype(BF)
        part_ref[c, 0:64] = nt(dhi_ref[c, 0:64], kernel)
        part_ref[c, 64:80] = nt(rows_of(x_ref, c, 80, 96), low_ref[c]) * 0.25
    for c in range(STEPS):
        query = rows_of(x_ref, c, 80, 96).astype(F32)
        own = nn(rows_of(x_ref, c, 0, 16), low_ref[c]) * 0.25
        dq_ref[c] = (pull(query, feat_ref[c], False) + own).astype(BF)


def query_grads(x, scores, pref, half, d_hi, d_lo):
    return pl.pallas_call(
        query_kernel,
        out_shape=(
            jax.ShapeDtypeStruct((STEPS, FD, WIDE), BF),
            jax.ShapeDtypeStruct((STEPS, ROWS, WIDE), F32),
        ),
        scratch_shapes=[
            pltpu.VMEM((STEPS, FEAT, WIDE), F32),
            pltpu.VMEM((STEPS, WIDE, WIDE), BF),
        ],
        compiler_params=PARAMS,
        name="query_grads",
    )(x, scores, pref, half, d_hi, d_lo)


def key_kernel(x_ref, lin_ref, dq_ref, part_ref, own_ref, half_ref, feat_ref, out_ref):
    run = half_ref[...]
    for c in range(STEPS - 1, -1, -1):
        key = rows_of(x_ref, c, 0, 16).astype(F32)
        ones = with_ones(rows_of(x_ref, c, 16, 80))
        feat = feat_ref[c]
        run_hi, run_lo = split(run)
        stack = nn(jnp.concatenate([run_hi[0:64], run_lo[0:64]], 0), feat)
        d_value = stack[0:64] + stack[64:128] + part_ref[c, 0:64]
        turned_hi, turned_lo = split(jnp.transpose(run))
        d_feat = nn(turned_hi, ones) + nn(turned_lo, ones)
        d_key = (pull(key, d_feat, True) + part_ref[c, 64:80]).astype(BF)
        d_value = d_value.astype(BF)
        for i in range(2):
            cols = slice(i * TOK, (i + 1) * TOK)
            out_ref[2 * c + i, 0:64] = lin_ref[c, :, cols]
            out_ref[2 * c + i, 64:80] = dq_ref[c, :, cols]
            out_ref[2 * c + i, 80:144] = d_value[:, cols]
            out_ref[2 * c + i, 144:160] = d_key[:, cols]
        if c:
            run = run + own_ref[c]


def key_grads(x, lin, dq, part, own, half, feat):
    return pl.pallas_call(
        key_kernel,
        out_shape=jax.ShapeDtypeStruct((H, 2 * ROWS, TOK), BF),
        compiler_params=PARAMS,
        name="key_grads",
    )(x, lin, dq, part, own, half, feat)


def window_kernel(
    first_ref, q_hbm, k_hbm, v_hbm, g_hbm, halo_ref,
    out_ref, dq_ref, dk_ref, dv_ref, back_ref,
    q_ref, k_ref, v_ref, g_ref, logit_ref, d_attn_ref, low_ref, d_low_ref, sems,
):
    copies = []
    pairs_in = ((k_hbm, k_ref), (q_hbm, q_ref), (v_hbm, v_ref), (g_hbm, g_ref))
    for i, (source, target) in enumerate(pairs_in):
        copies.append(pltpu.make_async_copy(source, target, sems.at[i]))
        copies[i].start()
    source = lax.broadcasted_iota(jnp.int32, (TOK, 2 * TOK), 0)
    target = lax.broadcasted_iota(jnp.int32, (TOK, 2 * TOK), 1) % TOK
    own = source <= target
    own_low = own.astype(F32).astype(BF)
    prev_low = (1.0 - own.astype(F32)).astype(BF)
    row = lax.broadcasted_iota(jnp.int32, (TOK, TOK), 0)
    col = lax.broadcasted_iota(jnp.int32, (TOK, TOK), 1)
    own_t = (col <= row).astype(F32).astype(BF)
    prev_t = (col > row).astype(F32).astype(BF)
    lane_a = (col < DH).astype(F32).astype(BF)
    lane_b = (col >= DH).astype(F32).astype(BF)
    blocked = jnp.where(first_ref[0] == 1, -1e30, 0.0)

    lane_a8 = lane_a * 0.125
    lane_b8 = lane_b * 0.125
    wide_a = jnp.concatenate([lane_a, lane_a], 0)
    wide_b = jnp.concatenate([lane_b, lane_b], 0)
    wide_a8 = jnp.concatenate([lane_a8, lane_a8], 0)
    wide_b8 = jnp.concatenate([lane_b8, lane_b8], 0)

    pairs = range(H // 2)

    def cols_of(p):
        return slice(p * 128, (p + 1) * 128)

    def query_rows(p):
        query = q_ref[:, cols_of(p)]
        return jnp.concatenate([query * lane_a8, query * lane_b8], 0)

    def grad_rows(p):
        grad = g_ref[:, cols_of(p)]
        return jnp.concatenate([grad * lane_a, grad * lane_b], 0)

    def key_rows(p):
        return jnp.concatenate([k_ref[:, cols_of(p)], halo_ref[0, :, cols_of(p)]], 0)

    def value_rows(p):
        return jnp.concatenate([v_ref[:, cols_of(p)], halo_ref[1, :, cols_of(p)]], 0)

    copies[0].wait()
    copies[1].wait()
    for p in pairs:
        scores = nt(key_rows(p), query_rows(p))
        logit_ref[p] = jnp.where(own, scores[0:TOK], scores[TOK:] + blocked)
    copies[2].wait()
    copies[3].wait()
    for p in pairs:
        d_both = nt(value_rows(p), grad_rows(p))
        d_attn_ref[p] = jnp.where(own, d_both[0:TOK], d_both[TOK:])
    for p in pairs:
        logits = logit_ref[p]
        shifted = jnp.exp(logits - jnp.max(logits, 0, keepdims=True))
        attn = shifted * (1.0 / jnp.sum(shifted, 0, keepdims=True))
        logit_ref[p] = attn
        low_ref[p] = attn.astype(BF)
    for p in pairs:
        pieces = []
        for i in range(2):
            turned = flip(low_ref[p, :, i * TOK : (i + 1) * TOK])
            pieces += [turned * own_t, turned * prev_t]
        values = value_rows(p)
        result = nn(
            jnp.concatenate(pieces, 1), jnp.concatenate([values * wide_a, values * wide_b], 0)
        )
        out_ref[:, cols_of(p)] = result
    for p in pairs:
        inner_t = jnp.transpose(out_ref[:, cols_of(p)] * g_ref[:, cols_of(p)].astype(F32))
        inner = jnp.concatenate(
            [jnp.sum(inner_t[0:64], 0, keepdims=True), jnp.sum(inner_t[64:128], 0, keepdims=True)],
            1,
        )
        d_low_ref[p] = (logit_ref[p] * (d_attn_ref[p] - inner)).astype(BF)
    for p in pairs:
        cols = cols_of(p)
        d_logits, attn_low = d_low_ref[p], low_ref[p]
        pieces = []
        for i in range(2):
            turned = flip(d_logits[:, i * TOK : (i + 1) * TOK])
            pieces += [turned * own_t, turned * prev_t]
        keys = key_rows(p)
        dq_ref[:, cols] = nn(
            jnp.concatenate(pieces, 1), jnp.concatenate([keys * wide_a8, keys * wide_b8], 0)
        ).astype(BF)
        d_keys = nn(jnp.concatenate([d_logits * own_low, d_logits * prev_low], 0), query_rows(p))
        dk_ref[:, cols] = d_keys[0:TOK]
        back_ref[0, :, cols] = d_keys[TOK:].astype(BF)
        d_values = nn(jnp.concatenate([attn_low * own_low, attn_low * prev_low], 0), grad_rows(p))
        dv_ref[:, cols] = d_values[0:TOK]
        back_ref[1, :, cols] = d_values[TOK:].astype(BF)


def window(first, q, k, v, g, halo):
    wide = (TOK, H * DH)
    hbm = pl.BlockSpec(memory_space=pltpu.HBM)
    return pl.pallas_call(
        window_kernel,
        in_specs=[pl.BlockSpec(memory_space=pltpu.SMEM)] + [hbm] * 4 + [pl.BlockSpec()],
        out_specs=(pl.BlockSpec(),) * 5,
        out_shape=(
            jax.ShapeDtypeStruct(wide, F32),
            jax.ShapeDtypeStruct(wide, BF),
            jax.ShapeDtypeStruct(wide, F32),
            jax.ShapeDtypeStruct(wide, F32),
            jax.ShapeDtypeStruct((2,) + wide, BF),
        ),
        scratch_shapes=[
            pltpu.VMEM(wide, BF),
            pltpu.VMEM(wide, BF),
            pltpu.VMEM(wide, BF),
            pltpu.VMEM(wide, BF),
            pltpu.VMEM((8, TOK, 2 * TOK), F32),
            pltpu.VMEM((8, TOK, 2 * TOK), F32),
            pltpu.VMEM((8, TOK, 2 * TOK), BF),
            pltpu.VMEM((8, TOK, 2 * TOK), BF),
            pltpu.SemaphoreType.DMA((4,)),
        ],
        compiler_params=PARAMS,
        cost_estimate=pl.CostEstimate(
            flops=5_000_000_000, transcendentals=0, bytes_accessed=6_000_000
        ),
        name="window",
    )(first, *(pltpu.with_memory_space_constraint(a, pltpu.HBM) for a in (q, k, v, g)), halo)


def settle_kernel(dk_ref, dv_ref, halo_ref, gkw_ref, sum_ref):
    gkw_ref[...] = (dk_ref[...] + halo_ref[0].astype(F32)).astype(BF)
    sum_ref[...] = dv_ref[...] + halo_ref[1].astype(F32)


def settle(dk, dv, halo):
    wide = (TOK, H * DH)
    return pl.pallas_call(
        settle_kernel,
        out_shape=(jax.ShapeDtypeStruct(wide, BF), jax.ShapeDtypeStruct(wide, F32)),
        compiler_params=PARAMS,
        cost_estimate=pl.CostEstimate(
            flops=50_000_000_000, transcendentals=0, bytes_accessed=2_000_000
        ),
        name="settle",
    )(dk, dv, halo)


def finish_kernel(y_ref, out_ref, dv_ref, mixed_ref, gq_ref, gk_ref, gv_ref):
    for p in range(8):
        cols = slice(p * 128, (p + 1) * 128)
        for ref, add_ref, row in ((mixed_ref, out_ref, 0), (gv_ref, dv_ref, 80)):
            pair = jnp.concatenate(
                [y_ref[2 * p, row : row + 64], y_ref[2 * p + 1, row : row + 64]], 0
            )
            ref[:, cols] = (flip(pair).astype(F32) + add_ref[:, cols]).astype(BF)
    for j in range(2):
        cols = slice(j * 128, (j + 1) * 128)
        for ref, row in ((gq_ref, 64), (gk_ref, 144)):
            ref[:, cols] = flip(
                jnp.concatenate([y_ref[8 * j + i, row : row + 16] for i in range(8)], 0)
            )


def finish(y, out, dv):
    wide = jax.ShapeDtypeStruct((TOK, H * DH), BF)
    thin = jax.ShapeDtypeStruct((TOK, H * FD), BF)
    return pl.pallas_call(
        finish_kernel,
        out_shape=(wide, thin, thin, wide),
        compiler_params=PARAMS,
        name="finish",
    )(y, out, dv)


def local(q_lin, k_lin, q_win, k_win, values, grad_out):
    seq = ("half", "head")
    spread = functools.partial(
        lax.all_to_all, axis_name="head", split_axis=0, concat_axis=0, tiled=True
    )
    later = [(i, i + 1) for i in range(31)]
    earlier = [(i + 1, i) for i in range(31)]
    own, halo = pack(q_lin, k_lin, k_win, values, grad_out)
    halo = lax.ppermute(halo, seq, later)
    x = spread(own)
    first = (lax.axis_index(seq) == 0).astype(jnp.int32).reshape(1)
    pref, total, key_feat = key_state(x)
    half = lax.ppermute(total, "half", [(0, 1)])
    scores, numer, query_feat = inside(x)
    numer, half = lax.optimization_barrier((numer, half))
    lin, d_hi, d_lo, state, total = output(x, pref, half, numer, query_feat)
    next_half = lax.ppermute(total, "half", [(1, 0)])
    d_hi, halo = lax.optimization_barrier((d_hi, halo))
    out, dq_win, dk, dv, back_halo = window(first, q_win, k_win, values, grad_out, halo)
    d_hi, back_halo, next_half = lax.optimization_barrier((d_hi, back_halo, next_half))
    back_halo = lax.ppermute(back_halo, seq, earlier)
    dq, part = query_grads(x, scores, pref, half, d_hi, d_lo)
    y = spread(key_grads(x, lin, dq, part, state, next_half, key_feat))
    gkw, dv = settle(dk, dv, back_halo)
    y, gkw, dv = lax.optimization_barrier((y, gkw, dv))
    mixed, gq, gk, gv = finish(y, out, dv)
    return (mixed, gq, gk, dq_win, gkw, gv)


def solution(mesh):
    inner = Mesh(mesh.devices.reshape(8, 2, 16), ("dp", "half", "head"))
    placed = P(("dp", "half", "head"), None)
    return jax.shard_map(
        local, mesh=inner, in_specs=(placed,) * 6, out_specs=(placed,) * 6, check_vma=False
    )
```

```python
import functools

import jax
import jax.numpy as jnp
from jax import lax
from jax.experimental import pallas as pl
from jax.experimental.pallas import tpu as pltpu
from jax.sharding import Mesh, PartitionSpec as P

H = 16
DH = 64
FD = 16
TOK = 128
FEAT = 224
ROWS = 80
WIDE = 256
STEPS = 8
BF = jnp.bfloat16
F32 = jnp.float32
PARAMS = pltpu.CompilerParams(vmem_limit_bytes=16 * 1024 * 1024)


def nn(a, b):
    return lax.dot_general(a, b, (((1,), (0,)), ((), ())), preferred_element_type=F32)


def nt(a, b):
    return lax.dot_general(a, b, (((1,), (1,)), ((), ())), preferred_element_type=F32)


def split(x):
    high = x.astype(BF)
    return high, (x - high.astype(F32)).astype(BF)


def flip(x):
    return jnp.transpose(x)


def pack_kernel(
    ql_hbm, kl_hbm, kw_hbm, v_hbm, g_hbm, out_ref, halo_hbm,
    ql_ref, kl_ref, kw_ref, v_ref, g_ref, sems,
):
    def copy(source, target, i):
        job = pltpu.make_async_copy(source, target, sems.at[i])
        job.start()
        return job

    value_in = copy(v_hbm, v_ref, 0)
    window_in = copy(kw_hbm, kw_ref, 1)
    grad_in = copy(g_hbm, g_ref, 2)
    key_in = copy(kl_hbm, kl_ref, 3)
    query_in = copy(ql_hbm, ql_ref, 4)
    value_in.wait()
    value_out = copy(v_ref, halo_hbm.at[1], 5)
    window_in.wait()
    window_out = copy(kw_ref, halo_hbm.at[0], 6)

    def wide(ref, base):
        for p in range(8):
            part = flip(ref[:, p * 128 : (p + 1) * 128])
            out_ref[2 * p, base : base + 64, :] = part[0:64]
            out_ref[2 * p + 1, base : base + 64, :] = part[64:128]

    def thin(ref, base):
        for j in range(2):
            part = flip(ref[:, j * 128 : (j + 1) * 128])
            for i in range(8):
                out_ref[8 * j + i, base : base + 16, :] = part[16 * i : 16 * i + 16]

    wide(v_ref, 16)
    grad_in.wait()
    wide(g_ref, 96)
    key_in.wait()
    thin(kl_ref, 0)
    query_in.wait()
    thin(ql_ref, 80)
    value_out.wait()
    window_out.wait()


def pack(q_lin, k_lin, k_win, values, grad_out):
    hbm = pl.BlockSpec(memory_space=pltpu.HBM)
    return pl.pallas_call(
        pack_kernel,
        in_specs=[hbm] * 5,
        out_specs=(pl.BlockSpec(memory_space=pltpu.VMEM), hbm),
        out_shape=(
            jax.ShapeDtypeStruct((H, 2 * ROWS, TOK), BF),
            jax.ShapeDtypeStruct((2, TOK, H * DH), BF),
        ),
        scratch_shapes=[
            pltpu.VMEM((TOK, H * FD), BF),
            pltpu.VMEM((TOK, H * FD), BF),
            pltpu.VMEM((TOK, H * DH), BF),
            pltpu.VMEM((TOK, H * DH), BF),
            pltpu.VMEM((TOK, H * DH), BF),
            pltpu.SemaphoreType.DMA((7,)),
        ],
        compiler_params=pltpu.CompilerParams(vmem_limit_bytes=60 * 1024 * 1024),
        name="pack",
    )(q_lin, k_lin, k_win, values, grad_out)


def features(x, square=1.0, cross=1.0, linear=1.0):
    low, up = x[0:8], x[8:16]
    left, mix, right = low * square, up * cross, up * square
    pieces = []
    for i in range(8):
        row = x[i : i + 1]
        pieces += [row * left, row * mix]
    for i in range(8, 16):
        pieces.append(x[i : i + 1] * right)
    pieces += [low * linear, up * linear]
    one = (lax.broadcasted_iota(jnp.int32, (8, x.shape[1]), 0) == 0).astype(F32)
    pieces += [one, jnp.zeros_like(one)]
    return jnp.concatenate(pieces, 0).astype(BF)


def pull(x, grad, weight):
    low, up = x[0:8], x[8:16]
    row_id = lax.broadcasted_iota(jnp.int32, low.shape, 0)
    acc_low = jnp.zeros_like(low)
    acc_mix = jnp.zeros_like(low)
    acc_up = jnp.zeros_like(low)
    red = jnp.zeros_like(low)
    for i in range(8):
        row = x[i : i + 1]
        own = grad[16 * i : 16 * i + 8]
        mix = grad[16 * i + 8 : 16 * i + 16]
        acc_low = acc_low + row * own
        acc_mix = acc_mix + row * mix
        red = jnp.where(row_id == i, jnp.sum(up * mix, 0, keepdims=True), red)
    for i in range(8, 16):
        acc_up = acc_up + x[i : i + 1] * grad[128 + 8 * (i - 8) : 136 + 8 * (i - 8)]
    if weight:
        out_low = (acc_low + red) * (1.0 / 16.0) + grad[192:200] * 0.25
        out_up = (acc_mix + acc_up) * (1.0 / 16.0) + grad[200:208] * 0.25
    else:
        out_low = 2.0 * acc_low + red + grad[192:200]
        out_up = acc_mix + 2.0 * acc_up + grad[200:208]
    return jnp.concatenate([out_low, out_up], 0)


def rows_of(ref, c, start, stop):
    return jnp.concatenate([ref[2 * c, start:stop], ref[2 * c + 1, start:stop]], 1)


def with_ones(v):
    tail = (lax.broadcasted_iota(jnp.int32, (16, v.shape[1]), 0) == 0).astype(BF)
    return jnp.concatenate([v, tail], 0)


def state_kernel(x_ref, pref_ref, total_ref, feat_ref):
    run = jnp.zeros((ROWS, FEAT), F32)
    for c in range(STEPS):
        pref_ref[c] = run
        key = rows_of(x_ref, c, 0, 16).astype(F32)
        feat = features(key, 1.0 / 32.0, 1.0 / 16.0, 0.25)
        feat_ref[c] = feat
        ones = with_ones(rows_of(x_ref, c, 16, 80))
        run = run + nt(ones, feat)
    total_ref[...] = run.astype(BF)


def key_state(x):
    feat = jax.ShapeDtypeStruct((STEPS, FEAT, WIDE), BF)
    return pl.pallas_call(
        state_kernel,
        out_shape=(
            jax.ShapeDtypeStruct((STEPS, ROWS, FEAT), F32),
            jax.ShapeDtypeStruct((ROWS, FEAT), BF),
            feat,
        ),
        compiler_params=PARAMS,
        name="key_state",
    )(x)


def causal_mask():
    source = lax.broadcasted_iota(jnp.int32, (WIDE, WIDE), 0)
    target = lax.broadcasted_iota(jnp.int32, (WIDE, WIDE), 1)
    return source <= target


def inside_kernel(x_ref, scores_ref, numer_ref, feat_ref):
    causal = causal_mask()
    for c in range(STEPS):
        key = rows_of(x_ref, c, 0, 16)
        query = rows_of(x_ref, c, 80, 96)
        ones = with_ones(rows_of(x_ref, c, 16, 80))
        scores = nn(flip(key), query) * 0.25
        scores_ref[c] = scores
        kernel_hi, kernel_lo = split(
            jnp.where(causal, 1.0 + scores + 0.5 * scores * scores, 0.0)
        )
        numer_ref[c] = nn(ones, kernel_hi) + nn(ones, kernel_lo)
        feat_ref[c] = features(query.astype(F32))


def inside(x):
    feat = jax.ShapeDtypeStruct((STEPS, FEAT, WIDE), BF)
    return pl.pallas_call(
        inside_kernel,
        out_shape=(
            jax.ShapeDtypeStruct((STEPS, WIDE, WIDE), F32),
            jax.ShapeDtypeStruct((STEPS, ROWS, WIDE), F32),
            feat,
        ),
        compiler_params=PARAMS,
        name="inside_chunks",
    )(x)


def output_kernel(
    x_ref, pref_ref, half_ref, numer_ref, feat_ref,
    lin_ref, dhi_ref, dlo_ref, own_ref, total_ref,
):
    total = jnp.zeros((ROWS, FEAT), F32)
    first = lax.broadcasted_iota(jnp.int32, (16, WIDE), 0) == 0
    for c in range(STEPS):
        grads = rows_of(x_ref, c, 96, 160).astype(F32)
        feat = feat_ref[c]
        state_hi, state_lo = split(pref_ref[c] + half_ref[...].astype(F32))
        stack = nn(jnp.concatenate([state_hi, state_lo], 0), feat)
        numer = numer_ref[c] + stack[0:ROWS] + stack[ROWS:]
        inv = 1.0 / numer[64:65]
        lin_out = numer[0:64] * inv
        d_denom = -jnp.sum(grads * lin_out, 0, keepdims=True) * inv
        d_hi, d_lo = split(
            jnp.concatenate([grads * inv, jnp.where(first, d_denom, 0.0)], 0)
        )
        stack = nt(jnp.concatenate([d_hi, d_lo], 0), feat)
        own = stack[0:ROWS] + stack[ROWS:]
        own_ref[c] = own
        total = total + own
        lin_ref[c] = lin_out.astype(BF)
        dhi_ref[c] = d_hi
        dlo_ref[c] = d_lo
    total_ref[...] = total.astype(BF)


def output(x, pref, half, numer, feat):
    side = jax.ShapeDtypeStruct((STEPS, ROWS, WIDE), BF)
    return pl.pallas_call(
        output_kernel,
        out_shape=(
            jax.ShapeDtypeStruct((STEPS, DH, WIDE), BF),
            side,
            side,
            jax.ShapeDtypeStruct((STEPS, ROWS, FEAT), F32),
            jax.ShapeDtypeStruct((ROWS, FEAT), BF),
        ),
        compiler_params=PARAMS,
        name="linear_output",
    )(x, pref, half, numer, feat)


def query_kernel(
    x_ref, scores_ref, pref_ref, half_ref, dhi_ref, dlo_ref, dq_ref, part_ref,
    feat_ref, low_ref,
):
    causal = causal_mask()
    for c in range(STEPS):
        d_hi, d_lo = dhi_ref[c], dlo_ref[c]
        ones_t = flip(with_ones(rows_of(x_ref, c, 16, 80)))
        d_kernel = nn(ones_t, d_hi) + nn(ones_t, d_lo)
        low_ref[c] = jnp.where(causal, d_kernel * (1.0 + scores_ref[c]), 0.0).astype(BF)
    for c in range(STEPS):
        d_hi, d_lo = dhi_ref[c], dlo_ref[c]
        turned_hi, turned_lo = split(jnp.transpose(pref_ref[c] + half_ref[...].astype(F32)))
        feat_ref[c] = nn(turned_hi, d_hi) + nn(turned_lo, d_hi) + nn(turned_hi, d_lo)
    for c in range(STEPS):
        scores = scores_ref[c]
        kernel = jnp.where(causal, 1.0 + scores + 0.5 * scores * scores, 0.0).astype(BF)
        part_ref[c, 0:64] = nt(dhi_ref[c, 0:64], kernel)
        part_ref[c, 64:80] = nt(rows_of(x_ref, c, 80, 96), low_ref[c]) * 0.25
    for c in range(STEPS):
        query = rows_of(x_ref, c, 80, 96).astype(F32)
        own = nn(rows_of(x_ref, c, 0, 16), low_ref[c]) * 0.25
        dq_ref[c] = (pull(query, feat_ref[c], False) + own).astype(BF)


def query_grads(x, scores, pref, half, d_hi, d_lo):
    return pl.pallas_call(
        query_kernel,
        out_shape=(
            jax.ShapeDtypeStruct((STEPS, FD, WIDE), BF),
            jax.ShapeDtypeStruct((STEPS, ROWS, WIDE), F32),
        ),
        scratch_shapes=[
            pltpu.VMEM((STEPS, FEAT, WIDE), F32),
            pltpu.VMEM((STEPS, WIDE, WIDE), BF),
        ],
        compiler_params=PARAMS,
        name="query_grads",
    )(x, scores, pref, half, d_hi, d_lo)


def key_kernel(x_ref, lin_ref, dq_ref, part_ref, own_ref, half_ref, feat_ref, out_ref):
    run = half_ref[...].astype(F32)
    for c in range(STEPS - 1, -1, -1):
        key = rows_of(x_ref, c, 0, 16).astype(F32)
        ones = with_ones(rows_of(x_ref, c, 16, 80))
        feat = feat_ref[c]
        run_hi, run_lo = split(run)
        stack = nn(jnp.concatenate([run_hi[0:64], run_lo[0:64]], 0), feat)
        d_value = stack[0:64] + stack[64:128] + part_ref[c, 0:64]
        turned_hi, turned_lo = split(jnp.transpose(run))
        d_feat = nn(turned_hi, ones) + nn(turned_lo, ones)
        d_key = (pull(key, d_feat, True) + part_ref[c, 64:80]).astype(BF)
        d_value = d_value.astype(BF)
        for i in range(2):
            cols = slice(i * TOK, (i + 1) * TOK)
            out_ref[2 * c + i, 0:64] = lin_ref[c, :, cols]
            out_ref[2 * c + i, 64:80] = dq_ref[c, :, cols]
            out_ref[2 * c + i, 80:144] = d_value[:, cols]
            out_ref[2 * c + i, 144:160] = d_key[:, cols]
        if c:
            run = run + own_ref[c]


def key_grads(x, lin, dq, part, own, half, feat):
    return pl.pallas_call(
        key_kernel,
        out_shape=jax.ShapeDtypeStruct((H, 2 * ROWS, TOK), BF),
        compiler_params=PARAMS,
        name="key_grads",
    )(x, lin, dq, part, own, half, feat)


def window_kernel(
    first_ref, q_hbm, k_hbm, v_hbm, g_hbm, halo_ref,
    out_ref, dq_ref, dk_ref, dv_ref, back_ref,
    q_ref, k_ref, v_ref, g_ref, logit_ref, d_attn_ref, low_ref, d_low_ref, sems,
):
    copies = []
    pairs_in = ((k_hbm, k_ref), (q_hbm, q_ref), (v_hbm, v_ref), (g_hbm, g_ref))
    for i, (source, target) in enumerate(pairs_in):
        copies.append(pltpu.make_async_copy(source, target, sems.at[i]))
        copies[i].start()
    source = lax.broadcasted_iota(jnp.int32, (TOK, 2 * TOK), 0)
    target = lax.broadcasted_iota(jnp.int32, (TOK, 2 * TOK), 1) % TOK
    own = source <= target
    own_low = own.astype(F32).astype(BF)
    prev_low = (1.0 - own.astype(F32)).astype(BF)
    row = lax.broadcasted_iota(jnp.int32, (TOK, TOK), 0)
    col = lax.broadcasted_iota(jnp.int32, (TOK, TOK), 1)
    own_t = (col <= row).astype(F32).astype(BF)
    prev_t = (col > row).astype(F32).astype(BF)
    lane_a = (col < DH).astype(F32).astype(BF)
    lane_b = (col >= DH).astype(F32).astype(BF)
    blocked = jnp.where(first_ref[0] == 1, -1e30, 0.0)

    lane_a8 = lane_a * 0.125
    lane_b8 = lane_b * 0.125
    wide_a = jnp.concatenate([lane_a, lane_a], 0)
    wide_b = jnp.concatenate([lane_b, lane_b], 0)
    wide_a8 = jnp.concatenate([lane_a8, lane_a8], 0)
    wide_b8 = jnp.concatenate([lane_b8, lane_b8], 0)

    pairs = range(H // 2)

    def cols_of(p):
        return slice(p * 128, (p + 1) * 128)

    def query_rows(p):
        query = q_ref[:, cols_of(p)]
        return jnp.concatenate([query * lane_a8, query * lane_b8], 0)

    def grad_rows(p):
        grad = g_ref[:, cols_of(p)]
        return jnp.concatenate([grad * lane_a, grad * lane_b], 0)

    def key_rows(p):
        return jnp.concatenate([k_ref[:, cols_of(p)], halo_ref[0, :, cols_of(p)]], 0)

    def value_rows(p):
        return jnp.concatenate([v_ref[:, cols_of(p)], halo_ref[1, :, cols_of(p)]], 0)

    copies[0].wait()
    copies[1].wait()
    for p in pairs:
        scores = nt(key_rows(p), query_rows(p))
        logit_ref[p] = jnp.where(own, scores[0:TOK], scores[TOK:] + blocked)
    copies[2].wait()
    copies[3].wait()
    for p in pairs:
        d_both = nt(value_rows(p), grad_rows(p))
        d_attn_ref[p] = jnp.where(own, d_both[0:TOK], d_both[TOK:])
    for p in pairs:
        logits = logit_ref[p]
        shifted = jnp.exp(logits - jnp.max(logits, 0, keepdims=True))
        attn = shifted * (1.0 / jnp.sum(shifted, 0, keepdims=True))
        logit_ref[p] = attn
        low_ref[p] = attn.astype(BF)
    for p in pairs:
        pieces = []
        for i in range(2):
            turned = flip(low_ref[p, :, i * TOK : (i + 1) * TOK])
            pieces += [turned * own_t, turned * prev_t]
        values = value_rows(p)
        result = nn(
            jnp.concatenate(pieces, 1), jnp.concatenate([values * wide_a, values * wide_b], 0)
        )
        out_ref[:, cols_of(p)] = result
    for p in pairs:
        inner_t = jnp.transpose(out_ref[:, cols_of(p)] * g_ref[:, cols_of(p)].astype(F32))
        inner = jnp.concatenate(
            [jnp.sum(inner_t[0:64], 0, keepdims=True), jnp.sum(inner_t[64:128], 0, keepdims=True)],
            1,
        )
        d_low_ref[p] = (logit_ref[p] * (d_attn_ref[p] - inner)).astype(BF)
    for p in pairs:
        cols = cols_of(p)
        d_logits, attn_low = d_low_ref[p], low_ref[p]
        pieces = []
        for i in range(2):
            turned = flip(d_logits[:, i * TOK : (i + 1) * TOK])
            pieces += [turned * own_t, turned * prev_t]
        keys = key_rows(p)
        dq_ref[:, cols] = nn(
            jnp.concatenate(pieces, 1), jnp.concatenate([keys * wide_a8, keys * wide_b8], 0)
        ).astype(BF)
        d_keys = nn(jnp.concatenate([d_logits * own_low, d_logits * prev_low], 0), query_rows(p))
        dk_ref[:, cols] = d_keys[0:TOK]
        back_ref[0, :, cols] = d_keys[TOK:].astype(BF)
        d_values = nn(jnp.concatenate([attn_low * own_low, attn_low * prev_low], 0), grad_rows(p))
        dv_ref[:, cols] = d_values[0:TOK]
        back_ref[1, :, cols] = d_values[TOK:].astype(BF)


def window(first, q, k, v, g, halo):
    wide = (TOK, H * DH)
    hbm = pl.BlockSpec(memory_space=pltpu.HBM)
    return pl.pallas_call(
        window_kernel,
        in_specs=[pl.BlockSpec(memory_space=pltpu.SMEM)] + [hbm] * 4 + [pl.BlockSpec()],
        out_specs=(pl.BlockSpec(),) * 5,
        out_shape=(
            jax.ShapeDtypeStruct(wide, F32),
            jax.ShapeDtypeStruct(wide, BF),
            jax.ShapeDtypeStruct(wide, F32),
            jax.ShapeDtypeStruct(wide, F32),
            jax.ShapeDtypeStruct((2,) + wide, BF),
        ),
        scratch_shapes=[
            pltpu.VMEM(wide, BF),
            pltpu.VMEM(wide, BF),
            pltpu.VMEM(wide, BF),
            pltpu.VMEM(wide, BF),
            pltpu.VMEM((8, TOK, 2 * TOK), F32),
            pltpu.VMEM((8, TOK, 2 * TOK), F32),
            pltpu.VMEM((8, TOK, 2 * TOK), BF),
            pltpu.VMEM((8, TOK, 2 * TOK), BF),
            pltpu.SemaphoreType.DMA((4,)),
        ],
        compiler_params=PARAMS,
        cost_estimate=pl.CostEstimate(
            flops=5_000_000_000, transcendentals=0, bytes_accessed=6_000_000
        ),
        name="window",
    )(first, *(pltpu.with_memory_space_constraint(a, pltpu.HBM) for a in (q, k, v, g)), halo)


def settle_kernel(dk_ref, dv_ref, halo_ref, gkw_ref, sum_ref):
    gkw_ref[...] = (dk_ref[...] + halo_ref[0].astype(F32)).astype(BF)
    sum_ref[...] = dv_ref[...] + halo_ref[1].astype(F32)


def settle(dk, dv, halo):
    wide = (TOK, H * DH)
    return pl.pallas_call(
        settle_kernel,
        out_shape=(jax.ShapeDtypeStruct(wide, BF), jax.ShapeDtypeStruct(wide, F32)),
        compiler_params=PARAMS,
        cost_estimate=pl.CostEstimate(
            flops=50_000_000_000, transcendentals=0, bytes_accessed=2_000_000
        ),
        name="settle",
    )(dk, dv, halo)


def finish_kernel(y_ref, out_ref, dv_ref, mixed_ref, gq_ref, gk_ref, gv_ref):
    for p in range(8):
        cols = slice(p * 128, (p + 1) * 128)
        for ref, add_ref, row in ((mixed_ref, out_ref, 0), (gv_ref, dv_ref, 80)):
            pair = jnp.concatenate(
                [y_ref[2 * p, row : row + 64], y_ref[2 * p + 1, row : row + 64]], 0
            )
            ref[:, cols] = (flip(pair).astype(F32) + add_ref[:, cols]).astype(BF)
    for j in range(2):
        cols = slice(j * 128, (j + 1) * 128)
        for ref, row in ((gq_ref, 64), (gk_ref, 144)):
            ref[:, cols] = flip(
                jnp.concatenate([y_ref[8 * j + i, row : row + 16] for i in range(8)], 0)
            )


def finish(y, out, dv):
    wide = jax.ShapeDtypeStruct((TOK, H * DH), BF)
    thin = jax.ShapeDtypeStruct((TOK, H * FD), BF)
    return pl.pallas_call(
        finish_kernel,
        out_shape=(wide, thin, thin, wide),
        compiler_params=PARAMS,
        name="finish",
    )(y, out, dv)


def local(q_lin, k_lin, q_win, k_win, values, grad_out):
    seq = ("half", "head")
    spread = functools.partial(
        lax.all_to_all, axis_name="head", split_axis=0, concat_axis=0, tiled=True
    )
    later = [(i, i + 1) for i in range(31)]
    earlier = [(i + 1, i) for i in range(31)]
    own, halo = pack(q_lin, k_lin, k_win, values, grad_out)
    halo = lax.ppermute(halo, seq, later)
    x = spread(own)
    first = (lax.axis_index(seq) == 0).astype(jnp.int32).reshape(1)
    pref, total, key_feat = key_state(x)
    half = lax.ppermute(total, "half", [(0, 1)])
    scores, numer, query_feat = inside(x)
    numer, half = lax.optimization_barrier((numer, half))
    lin, d_hi, d_lo, state, total = output(x, pref, half, numer, query_feat)
    next_half = lax.ppermute(total, "half", [(1, 0)])
    d_hi, halo = lax.optimization_barrier((d_hi, halo))
    out, dq_win, dk, dv, back_halo = window(first, q_win, k_win, values, grad_out, halo)
    d_hi, back_halo, next_half = lax.optimization_barrier((d_hi, back_halo, next_half))
    back_halo = lax.ppermute(back_halo, seq, earlier)
    dq, part = query_grads(x, scores, pref, half, d_hi, d_lo)
    y = spread(key_grads(x, lin, dq, part, state, next_half, key_feat))
    gkw, dv = settle(dk, dv, back_halo)
    y, gkw, dv = lax.optimization_barrier((y, gkw, dv))
    mixed, gq, gk, gv = finish(y, out, dv)
    return (mixed, gq, gk, dq_win, gkw, gv)


def solution(mesh):
    inner = Mesh(mesh.devices.reshape(8, 2, 16), ("dp", "half", "head"))
    placed = P(("dp", "half", "head"), None)
    return jax.shard_map(
        local, mesh=inner, in_specs=(placed,) * 6, out_specs=(placed,) * 6, check_vma=False
    )
```

```python
import functools

import jax
import jax.numpy as jnp
from jax import lax
from jax.experimental import pallas as pl
from jax.experimental.pallas import tpu as pltpu
from jax.sharding import Mesh, PartitionSpec as P

H = 16
DH = 64
FD = 16
TOK = 128
FEAT = 224
ROWS = 80
WIDE = 256
STEPS = 8
BF = jnp.bfloat16
F32 = jnp.float32
PARAMS = pltpu.CompilerParams(vmem_limit_bytes=16 * 1024 * 1024)


def nn(a, b):
    return lax.dot_general(a, b, (((1,), (0,)), ((), ())), preferred_element_type=F32)


def nt(a, b):
    return lax.dot_general(a, b, (((1,), (1,)), ((), ())), preferred_element_type=F32)


def split(x):
    high = x.astype(BF)
    return high, (x - high.astype(F32)).astype(BF)


def flip(x):
    return jnp.transpose(x)


def pack_kernel(
    ql_hbm, kl_hbm, kw_hbm, v_hbm, g_hbm, out_ref, halo_hbm,
    ql_ref, kl_ref, kw_ref, v_ref, g_ref, sems,
):
    def copy(source, target, i):
        job = pltpu.make_async_copy(source, target, sems.at[i])
        job.start()
        return job

    value_in = copy(v_hbm, v_ref, 0)
    window_in = copy(kw_hbm, kw_ref, 1)
    grad_in = copy(g_hbm, g_ref, 2)
    key_in = copy(kl_hbm, kl_ref, 3)
    query_in = copy(ql_hbm, ql_ref, 4)
    value_in.wait()
    value_out = copy(v_ref, halo_hbm.at[1], 5)
    window_in.wait()
    window_out = copy(kw_ref, halo_hbm.at[0], 6)

    def wide(ref, base):
        for p in range(8):
            part = flip(ref[:, p * 128 : (p + 1) * 128])
            out_ref[2 * p, base : base + 64, :] = part[0:64]
            out_ref[2 * p + 1, base : base + 64, :] = part[64:128]

    def thin(ref, base):
        for j in range(2):
            part = flip(ref[:, j * 128 : (j + 1) * 128])
            for i in range(8):
                out_ref[8 * j + i, base : base + 16, :] = part[16 * i : 16 * i + 16]

    wide(v_ref, 16)
    grad_in.wait()
    wide(g_ref, 96)
    key_in.wait()
    thin(kl_ref, 0)
    query_in.wait()
    thin(ql_ref, 80)
    value_out.wait()
    window_out.wait()


def pack(q_lin, k_lin, k_win, values, grad_out):
    hbm = pl.BlockSpec(memory_space=pltpu.HBM)
    return pl.pallas_call(
        pack_kernel,
        in_specs=[hbm] * 5,
        out_specs=(pl.BlockSpec(memory_space=pltpu.VMEM), hbm),
        out_shape=(
            jax.ShapeDtypeStruct((H, 2 * ROWS, TOK), BF),
            jax.ShapeDtypeStruct((2, TOK, H * DH), BF),
        ),
        scratch_shapes=[
            pltpu.VMEM((TOK, H * FD), BF),
            pltpu.VMEM((TOK, H * FD), BF),
            pltpu.VMEM((TOK, H * DH), BF),
            pltpu.VMEM((TOK, H * DH), BF),
            pltpu.VMEM((TOK, H * DH), BF),
            pltpu.SemaphoreType.DMA((7,)),
        ],
        compiler_params=pltpu.CompilerParams(vmem_limit_bytes=60 * 1024 * 1024),
        name="pack",
    )(q_lin, k_lin, k_win, values, grad_out)


def features(x, square=1.0, cross=1.0, linear=1.0):
    low, up = x[0:8], x[8:16]
    left, mix, right = low * square, up * cross, up * square
    pieces = []
    for i in range(8):
        row = x[i : i + 1]
        pieces += [row * left, row * mix]
    for i in range(8, 16):
        pieces.append(x[i : i + 1] * right)
    pieces += [low * linear, up * linear]
    one = (lax.broadcasted_iota(jnp.int32, (8, x.shape[1]), 0) == 0).astype(F32)
    pieces += [one, jnp.zeros_like(one)]
    return jnp.concatenate(pieces, 0).astype(BF)


def pull(x, grad, weight):
    low, up = x[0:8], x[8:16]
    row_id = lax.broadcasted_iota(jnp.int32, low.shape, 0)
    acc_low = jnp.zeros_like(low)
    acc_mix = jnp.zeros_like(low)
    acc_up = jnp.zeros_like(low)
    red = jnp.zeros_like(low)
    for i in range(8):
        row = x[i : i + 1]
        own = grad[16 * i : 16 * i + 8]
        mix = grad[16 * i + 8 : 16 * i + 16]
        acc_low = acc_low + row * own
        acc_mix = acc_mix + row * mix
        red = jnp.where(row_id == i, jnp.sum(up * mix, 0, keepdims=True), red)
    for i in range(8, 16):
        acc_up = acc_up + x[i : i + 1] * grad[128 + 8 * (i - 8) : 136 + 8 * (i - 8)]
    if weight:
        out_low = (acc_low + red) * (1.0 / 16.0) + grad[192:200] * 0.25
        out_up = (acc_mix + acc_up) * (1.0 / 16.0) + grad[200:208] * 0.25
    else:
        out_low = 2.0 * acc_low + red + grad[192:200]
        out_up = acc_mix + 2.0 * acc_up + grad[200:208]
    return jnp.concatenate([out_low, out_up], 0)


def rows_of(ref, c, start, stop):
    return jnp.concatenate([ref[2 * c, start:stop], ref[2 * c + 1, start:stop]], 1)


def with_ones(v):
    tail = (lax.broadcasted_iota(jnp.int32, (16, v.shape[1]), 0) == 0).astype(BF)
    return jnp.concatenate([v, tail], 0)


def state_kernel(x_ref, pref_ref, total_ref, feat_ref):
    run = jnp.zeros((ROWS, FEAT), F32)
    for c in range(STEPS):
        pref_ref[c] = run
        key = rows_of(x_ref, c, 0, 16).astype(F32)
        feat = features(key, 1.0 / 32.0, 1.0 / 16.0, 0.25)
        feat_ref[c] = feat
        ones = with_ones(rows_of(x_ref, c, 16, 80))
        run = run + nt(ones, feat)
    total_ref[...] = run.astype(BF)


def key_state(x):
    feat = jax.ShapeDtypeStruct((STEPS, FEAT, WIDE), BF)
    return pl.pallas_call(
        state_kernel,
        out_shape=(
            jax.ShapeDtypeStruct((STEPS, ROWS, FEAT), F32),
            jax.ShapeDtypeStruct((ROWS, FEAT), BF),
            feat,
        ),
        compiler_params=PARAMS,
        name="key_state",
    )(x)


def causal_mask():
    source = lax.broadcasted_iota(jnp.int32, (WIDE, WIDE), 0)
    target = lax.broadcasted_iota(jnp.int32, (WIDE, WIDE), 1)
    return source <= target


def inside_kernel(x_ref, scores_ref, numer_ref, feat_ref):
    causal = causal_mask()
    for c in range(STEPS):
        key = rows_of(x_ref, c, 0, 16)
        query = rows_of(x_ref, c, 80, 96)
        ones = with_ones(rows_of(x_ref, c, 16, 80))
        scores = nn(flip(key), query) * 0.25
        scores_ref[c] = scores
        kernel_hi, kernel_lo = split(
            jnp.where(causal, 1.0 + scores + 0.5 * scores * scores, 0.0)
        )
        numer_ref[c] = nn(ones, kernel_hi) + nn(ones, kernel_lo)
        feat_ref[c] = features(query.astype(F32))


def inside(x):
    feat = jax.ShapeDtypeStruct((STEPS, FEAT, WIDE), BF)
    return pl.pallas_call(
        inside_kernel,
        out_shape=(
            jax.ShapeDtypeStruct((STEPS, WIDE, WIDE), F32),
            jax.ShapeDtypeStruct((STEPS, ROWS, WIDE), F32),
            feat,
        ),
        compiler_params=PARAMS,
        name="inside_chunks",
    )(x)


def output_kernel(
    x_ref, pref_ref, half_ref, numer_ref, feat_ref,
    lin_ref, dhi_ref, dlo_ref, own_ref, total_ref,
):
    total = jnp.zeros((ROWS, FEAT), F32)
    first = lax.broadcasted_iota(jnp.int32, (16, WIDE), 0) == 0
    for c in range(STEPS):
        grads = rows_of(x_ref, c, 96, 160).astype(F32)
        feat = feat_ref[c]
        state_hi, state_lo = split(pref_ref[c] + half_ref[...].astype(F32))
        stack = nn(jnp.concatenate([state_hi, state_lo], 0), feat)
        numer = numer_ref[c] + stack[0:ROWS] + stack[ROWS:]
        inv = 1.0 / numer[64:65]
        lin_out = numer[0:64] * inv
        d_denom = -jnp.sum(grads * lin_out, 0, keepdims=True) * inv
        d_hi, d_lo = split(
            jnp.concatenate([grads * inv, jnp.where(first, d_denom, 0.0)], 0)
        )
        stack = nt(jnp.concatenate([d_hi, d_lo], 0), feat)
        own = stack[0:ROWS] + stack[ROWS:]
        own_ref[c] = own
        total = total + own
        lin_ref[c] = lin_out.astype(BF)
        dhi_ref[c] = d_hi
        dlo_ref[c] = d_lo
    total_ref[...] = total.astype(BF)


def output(x, pref, half, numer, feat):
    side = jax.ShapeDtypeStruct((STEPS, ROWS, WIDE), BF)
    return pl.pallas_call(
        output_kernel,
        out_shape=(
            jax.ShapeDtypeStruct((STEPS, DH, WIDE), BF),
            side,
            side,
            jax.ShapeDtypeStruct((STEPS, ROWS, FEAT), F32),
            jax.ShapeDtypeStruct((ROWS, FEAT), BF),
        ),
        compiler_params=PARAMS,
        name="linear_output",
    )(x, pref, half, numer, feat)


def query_kernel(
    x_ref, scores_ref, pref_ref, half_ref, dhi_ref, dlo_ref, dq_ref, part_ref,
    feat_ref, low_ref,
):
    causal = causal_mask()
    for c in range(STEPS):
        d_hi, d_lo = dhi_ref[c], dlo_ref[c]
        ones_t = flip(with_ones(rows_of(x_ref, c, 16, 80)))
        d_kernel = nn(ones_t, d_hi) + nn(ones_t, d_lo)
        low_ref[c] = jnp.where(causal, d_kernel * (1.0 + scores_ref[c]), 0.0).astype(BF)
    for c in range(STEPS):
        d_hi, d_lo = dhi_ref[c], dlo_ref[c]
        turned_hi, turned_lo = split(jnp.transpose(pref_ref[c] + half_ref[...].astype(F32)))
        feat_ref[c] = nn(turned_hi, d_hi) + nn(turned_lo, d_hi) + nn(turned_hi, d_lo)
    for c in range(STEPS):
        scores = scores_ref[c]
        kernel = jnp.where(causal, 1.0 + scores + 0.5 * scores * scores, 0.0).astype(BF)
        part_ref[c, 0:64] = nt(dhi_ref[c, 0:64], kernel)
        part_ref[c, 64:80] = nt(rows_of(x_ref, c, 80, 96), low_ref[c]) * 0.25
    for c in range(STEPS):
        query = rows_of(x_ref, c, 80, 96).astype(F32)
        own = nn(rows_of(x_ref, c, 0, 16), low_ref[c]) * 0.25
        dq_ref[c] = (pull(query, feat_ref[c], False) + own).astype(BF)


def query_grads(x, scores, pref, half, d_hi, d_lo):
    return pl.pallas_call(
        query_kernel,
        out_shape=(
            jax.ShapeDtypeStruct((STEPS, FD, WIDE), BF),
            jax.ShapeDtypeStruct((STEPS, ROWS, WIDE), F32),
        ),
        scratch_shapes=[
            pltpu.VMEM((STEPS, FEAT, WIDE), F32),
            pltpu.VMEM((STEPS, WIDE, WIDE), BF),
        ],
        compiler_params=PARAMS,
        name="query_grads",
    )(x, scores, pref, half, d_hi, d_lo)


def key_kernel(x_ref, lin_ref, dq_ref, part_ref, own_ref, half_ref, feat_ref, out_hbm, out_ref, sems):
    copies = []
    run = half_ref[...].astype(F32)
    for c in range(STEPS - 1, -1, -1):
        key = rows_of(x_ref, c, 0, 16).astype(F32)
        ones = with_ones(rows_of(x_ref, c, 16, 80))
        feat = feat_ref[c]
        run_hi, run_lo = split(run)
        stack = nn(jnp.concatenate([run_hi[0:64], run_lo[0:64]], 0), feat)
        d_value = stack[0:64] + stack[64:128] + part_ref[c, 0:64]
        turned_hi, turned_lo = split(jnp.transpose(run))
        d_feat = nn(turned_hi, ones) + nn(turned_lo, ones)
        d_key = (pull(key, d_feat, True) + part_ref[c, 64:80]).astype(BF)
        d_value = d_value.astype(BF)
        for i in range(2):
            cols = slice(i * TOK, (i + 1) * TOK)
            out_ref[2 * c + i, 0:64] = lin_ref[c, :, cols]
            out_ref[2 * c + i, 64:80] = dq_ref[c, :, cols]
            out_ref[2 * c + i, 80:144] = d_value[:, cols]
            out_ref[2 * c + i, 144:160] = d_key[:, cols]
        rows = pl.ds(2 * c, 2)
        copies.append(pltpu.make_async_copy(out_ref.at[rows], out_hbm.at[rows], sems.at[c]))
        copies[-1].start()
        if c:
            run = run + own_ref[c]
    for copy in copies:
        copy.wait()


def key_grads(x, lin, dq, part, own, half, feat):
    return pl.pallas_call(
        key_kernel,
        out_specs=pl.BlockSpec(memory_space=pltpu.HBM),
        out_shape=jax.ShapeDtypeStruct((H, 2 * ROWS, TOK), BF),
        scratch_shapes=[
            pltpu.VMEM((H, 2 * ROWS, TOK), BF),
            pltpu.SemaphoreType.DMA((STEPS,)),
        ],
        compiler_params=PARAMS,
        name="key_grads",
    )(x, lin, dq, part, own, half, feat)


def window_kernel(
    first_ref, q_hbm, k_hbm, v_hbm, g_hbm, halo_ref,
    out_ref, dq_ref, dk_ref, dv_ref, back_ref,
    q_ref, k_ref, v_ref, g_ref, logit_ref, d_attn_ref, low_ref, d_low_ref, sems,
):
    copies = []
    pairs_in = ((k_hbm, k_ref), (q_hbm, q_ref), (v_hbm, v_ref), (g_hbm, g_ref))
    for i, (source, target) in enumerate(pairs_in):
        copies.append(pltpu.make_async_copy(source, target, sems.at[i]))
        copies[i].start()
    source = lax.broadcasted_iota(jnp.int32, (TOK, 2 * TOK), 0)
    target = lax.broadcasted_iota(jnp.int32, (TOK, 2 * TOK), 1) % TOK
    own = source <= target
    own_low = own.astype(F32).astype(BF)
    prev_low = (1.0 - own.astype(F32)).astype(BF)
    row = lax.broadcasted_iota(jnp.int32, (TOK, TOK), 0)
    col = lax.broadcasted_iota(jnp.int32, (TOK, TOK), 1)
    own_t = (col <= row).astype(F32).astype(BF)
    prev_t = (col > row).astype(F32).astype(BF)
    lane_a = (col < DH).astype(F32).astype(BF)
    lane_b = (col >= DH).astype(F32).astype(BF)
    blocked = jnp.where(first_ref[0] == 1, -1e30, 0.0)

    lane_a8 = lane_a * 0.125
    lane_b8 = lane_b * 0.125
    wide_a = jnp.concatenate([lane_a, lane_a], 0)
    wide_b = jnp.concatenate([lane_b, lane_b], 0)
    wide_a8 = jnp.concatenate([lane_a8, lane_a8], 0)
    wide_b8 = jnp.concatenate([lane_b8, lane_b8], 0)

    pairs = range(H // 2)

    def cols_of(p):
        return slice(p * 128, (p + 1) * 128)

    def query_rows(p):
        query = q_ref[:, cols_of(p)]
        return jnp.concatenate([query * lane_a8, query * lane_b8], 0)

    def grad_rows(p):
        grad = g_ref[:, cols_of(p)]
        return jnp.concatenate([grad * lane_a, grad * lane_b], 0)

    def key_rows(p):
        return jnp.concatenate([k_ref[:, cols_of(p)], halo_ref[0, :, cols_of(p)]], 0)

    def value_rows(p):
        return jnp.concatenate([v_ref[:, cols_of(p)], halo_ref[1, :, cols_of(p)]], 0)

    copies[0].wait()
    copies[1].wait()
    for p in pairs:
        scores = nt(key_rows(p), query_rows(p))
        logit_ref[p] = jnp.where(own, scores[0:TOK], scores[TOK:] + blocked)
    for p in pairs:
        logits = logit_ref[p]
        shifted = jnp.exp(logits - jnp.max(logits, 0, keepdims=True))
        attn = shifted * (1.0 / jnp.sum(shifted, 0, keepdims=True))
        logit_ref[p] = attn
        low_ref[p] = attn.astype(BF)
    copies[2].wait()
    copies[3].wait()
    for p in pairs:
        d_both = nt(value_rows(p), grad_rows(p))
        d_attn_ref[p] = jnp.where(own, d_both[0:TOK], d_both[TOK:])
    for p in pairs:
        pieces = []
        for i in range(2):
            turned = flip(low_ref[p, :, i * TOK : (i + 1) * TOK])
            pieces += [turned * own_t, turned * prev_t]
        values = value_rows(p)
        result = nn(
            jnp.concatenate(pieces, 1), jnp.concatenate([values * wide_a, values * wide_b], 0)
        )
        out_ref[:, cols_of(p)] = result
    for p in pairs:
        inner_t = jnp.transpose(out_ref[:, cols_of(p)] * g_ref[:, cols_of(p)].astype(F32))
        inner = jnp.concatenate(
            [jnp.sum(inner_t[0:64], 0, keepdims=True), jnp.sum(inner_t[64:128], 0, keepdims=True)],
            1,
        )
        d_low_ref[p] = (logit_ref[p] * (d_attn_ref[p] - inner)).astype(BF)
    for p in pairs:
        cols = cols_of(p)
        d_logits, attn_low = d_low_ref[p], low_ref[p]
        pieces = []
        for i in range(2):
            turned = flip(d_logits[:, i * TOK : (i + 1) * TOK])
            pieces += [turned * own_t, turned * prev_t]
        keys = key_rows(p)
        dq_ref[:, cols] = nn(
            jnp.concatenate(pieces, 1), jnp.concatenate([keys * wide_a8, keys * wide_b8], 0)
        ).astype(BF)
        d_keys = nn(jnp.concatenate([d_logits * own_low, d_logits * prev_low], 0), query_rows(p))
        dk_ref[:, cols] = d_keys[0:TOK]
        back_ref[0, :, cols] = d_keys[TOK:].astype(BF)
        d_values = nn(jnp.concatenate([attn_low * own_low, attn_low * prev_low], 0), grad_rows(p))
        dv_ref[:, cols] = d_values[0:TOK]
        back_ref[1, :, cols] = d_values[TOK:].astype(BF)


def window(first, q, k, v, g, halo):
    wide = (TOK, H * DH)
    hbm = pl.BlockSpec(memory_space=pltpu.HBM)
    return pl.pallas_call(
        window_kernel,
        in_specs=[pl.BlockSpec(memory_space=pltpu.SMEM)] + [hbm] * 4 + [pl.BlockSpec()],
        out_specs=(pl.BlockSpec(),) * 5,
        out_shape=(
            jax.ShapeDtypeStruct(wide, F32),
            jax.ShapeDtypeStruct(wide, BF),
            jax.ShapeDtypeStruct(wide, F32),
            jax.ShapeDtypeStruct(wide, F32),
            jax.ShapeDtypeStruct((2,) + wide, BF),
        ),
        scratch_shapes=[
            pltpu.VMEM(wide, BF),
            pltpu.VMEM(wide, BF),
            pltpu.VMEM(wide, BF),
            pltpu.VMEM(wide, BF),
            pltpu.VMEM((8, TOK, 2 * TOK), F32),
            pltpu.VMEM((8, TOK, 2 * TOK), F32),
            pltpu.VMEM((8, TOK, 2 * TOK), BF),
            pltpu.VMEM((8, TOK, 2 * TOK), BF),
            pltpu.SemaphoreType.DMA((4,)),
        ],
        compiler_params=PARAMS,
        cost_estimate=pl.CostEstimate(
            flops=5_000_000_000, transcendentals=0, bytes_accessed=6_000_000
        ),
        name="window",
    )(first, *(pltpu.with_memory_space_constraint(a, pltpu.HBM) for a in (q, k, v, g)), halo)


def settle_kernel(dk_ref, dv_ref, halo_ref, gkw_ref, sum_ref):
    gkw_ref[...] = (dk_ref[...] + halo_ref[0].astype(F32)).astype(BF)
    sum_ref[...] = dv_ref[...] + halo_ref[1].astype(F32)


def settle(dk, dv, halo):
    wide = (TOK, H * DH)
    return pl.pallas_call(
        settle_kernel,
        out_shape=(jax.ShapeDtypeStruct(wide, BF), jax.ShapeDtypeStruct(wide, F32)),
        compiler_params=PARAMS,
        cost_estimate=pl.CostEstimate(
            flops=50_000_000_000, transcendentals=0, bytes_accessed=2_000_000
        ),
        name="settle",
    )(dk, dv, halo)


def finish_kernel(y_ref, out_ref, dv_ref, mixed_ref, gq_ref, gk_ref, gv_ref):
    for p in range(8):
        cols = slice(p * 128, (p + 1) * 128)
        for ref, add_ref, row in ((mixed_ref, out_ref, 0), (gv_ref, dv_ref, 80)):
            pair = jnp.concatenate(
                [y_ref[2 * p, row : row + 64], y_ref[2 * p + 1, row : row + 64]], 0
            )
            ref[:, cols] = (flip(pair).astype(F32) + add_ref[:, cols]).astype(BF)
    for j in range(2):
        cols = slice(j * 128, (j + 1) * 128)
        for ref, row in ((gq_ref, 64), (gk_ref, 144)):
            ref[:, cols] = flip(
                jnp.concatenate([y_ref[8 * j + i, row : row + 16] for i in range(8)], 0)
            )


def finish(y, out, dv):
    wide = jax.ShapeDtypeStruct((TOK, H * DH), BF)
    thin = jax.ShapeDtypeStruct((TOK, H * FD), BF)
    return pl.pallas_call(
        finish_kernel,
        out_shape=(wide, thin, thin, wide),
        compiler_params=PARAMS,
        name="finish",
    )(y, out, dv)


def local(q_lin, k_lin, q_win, k_win, values, grad_out):
    seq = ("half", "head")
    spread = functools.partial(
        lax.all_to_all, axis_name="head", split_axis=0, concat_axis=0, tiled=True
    )
    later = [(i, i + 1) for i in range(31)]
    earlier = [(i + 1, i) for i in range(31)]
    own, halo = pack(q_lin, k_lin, k_win, values, grad_out)
    halo = lax.ppermute(halo, seq, later)
    x = spread(own)
    first = (lax.axis_index(seq) == 0).astype(jnp.int32).reshape(1)
    pref, total, key_feat = key_state(x)
    half = lax.ppermute(total, "half", [(0, 1)])
    scores, numer, query_feat = inside(x)
    numer, half = lax.optimization_barrier((numer, half))
    lin, d_hi, d_lo, state, total = output(x, pref, half, numer, query_feat)
    next_half = lax.ppermute(total, "half", [(1, 0)])
    d_hi, halo = lax.optimization_barrier((d_hi, halo))
    out, dq_win, dk, dv, back_halo = window(first, q_win, k_win, values, grad_out, halo)
    d_hi, back_halo, next_half = lax.optimization_barrier((d_hi, back_halo, next_half))
    back_halo = lax.ppermute(back_halo, seq, earlier)
    dq, part = query_grads(x, scores, pref, half, d_hi, d_lo)
    y = spread(key_grads(x, lin, dq, part, state, next_half, key_feat))
    gkw, dv = settle(dk, dv, back_halo)
    y, gkw, dv = lax.optimization_barrier((y, gkw, dv))
    mixed, gq, gk, gv = finish(y, out, dv)
    return (mixed, gq, gk, dq_win, gkw, gv)


def solution(mesh):
    inner = Mesh(mesh.devices.reshape(8, 2, 16), ("dp", "half", "head"))
    placed = P(("dp", "half", "head"), None)
    return jax.shard_map(
        local, mesh=inner, in_specs=(placed,) * 6, out_specs=(placed,) * 6, check_vma=False
    )
```
